32 devices in a mesh: groups: 2 (over x), dom: 8 (over z, y), mp: 2 (over core).
Axes of the slice: x: 2, y: 2, z: 4, core: 2. Of those that a mesh axis runs over, the one named last changes fastest.
Arguments:
- feats: bfloat16 [24576, 256], P(('groups', 'dom')), parts along dimension 0, may hold values from -6 to 6
- cell_count: int32 [16], P(('groups', 'dom')), parts along dimension 0, may hold values from 1 to 1536, 9216 in all
- tile_col: int32 [192, 8], P(('groups', 'dom')), parts along dimension 0, may hold values from 0 to 11, all different within a row
- tile_val: bfloat16 [192, 8, 128, 128], P(('groups', 'dom')), parts along dimension 0, may hold values from -0.1875 to 0.1875
- send_list: int32 [16, 8, 64], P(('groups', 'dom')), parts along dimension 0, may hold values from 0 to 1535
- send_count: int32 [16, 8], P(('groups', 'dom')), parts along dimension 0, may hold values from 1 to 64, 256 in all within a row
- recv_list: int32 [16, 8, 64], P(('groups', 'dom')), parts along dimension 0, may hold values from 0 to 1535
- gate_weight_matrix: bfloat16 [2, 256, 512], P(None, None, 'mp'), may hold values from -0.375 to 0.375
- w_up: bfloat16 [2, 256, 512], P(None, None, 'mp'), may hold values from -0.375 to 0.375
- w_down: bfloat16 [2, 512, 256], P(None, 'mp'), may hold values from -0.25 to 0.25
- out_grad: bfloat16 [24576, 256], P(('groups', 'dom')), parts along dimension 0, may hold values from -6 to 6
Outputs:
- final: bfloat16 [24576, 256], P(('groups', 'dom')), parts along dimension 0
- feat_grad: float32 [24576, 256], P(('groups', 'dom')), parts along dimension 0
- grad_gate: float32 [4, 256, 512], P('groups', None, 'mp'), parts along dimension 0
- grad_up: float32 [4, 256, 512], P('groups', None, 'mp'), parts along dimension 0
- down_weight_gradient: float32 [4, 512, 256], P('groups', 'mp'), parts along dimension 0
The draws below stay inside these ranges and needn't reach their ends.
There are 2 independent parts, one for each index of `groups`. The reference program is written for one: setup_inputs(seed, part) draws one part's arguments, and reference() takes and returns one part's arrays. A program takes and returns all parts, laid end to end along the dimension named above; an argument that names none is the same for every part. Nothing has to cross between parts.
Inputs may be any that keep to these rules, and one draw needn't show every extreme that they name: Partition p has live cells in its rows 0 to cell_count[p] - 1; some partition is full in every draw, and the counts sum to 9216. `tile_col`: the entries of one row block are distinct local block columns; every block column is named somewhere. `send_list`: slots at or past send_count are unused. `send_count`: entry [s, q] counts live slots from partition s to partition q, its own included; each row sums to 256 and its largest entry is exactly 64. `recv_list`: entry [q, s, k] is the receiver's local row fed by slot k from partition s.
All inputs are finite; a program needn't handle non-finite values. No bound on the sum of `cell_count` on one device may be relied on, other than what follows from the above.
Results may differ from the reference program's by a relative error of at most 0.03.
Values may be sent and summed in bfloat16 or wider, within the bound.
No kernel may reach another device: no remote copies, remote signals or barrier semaphores. Data moves between devices by JAX's collectives and lax.ppermute only.
A program may use at most 128 MiB of HBM per device.

```python
import math
import jax
import jax.numpy as jnp
import numpy as np
from jax import lax

F = 256
H = 512
C_DEV = 1536
NB = 8
CAP = 64
L = 2
CELLS = 12288
N_DOM = 8


def place_ends(drawn, key, least, top_value):
    index_at = [jax.random.randint(jax.random.fold_in(key, axis), (), 0, length) for axis, length in enumerate(drawn.shape)]
    longest = drawn.shape.index(max(drawn.shape))
    beside = index_at[:longest] + [(index_at[longest] + 1) % drawn.shape[longest]] + index_at[longest + 1:]
    return drawn.at[tuple(index_at)].set(least).at[tuple(beside)].set(top_value)


def block_scale(own_key, dims, shards, least, top_value):
    def one(dim, blocks):
        draws = jax.random.uniform(jax.random.fold_in(jax.random.fold_in(own_key, 6), dim), (blocks,), jnp.float32, least / len(shards), top_value / len(shards))
        return jnp.repeat(jnp.exp(draws), dims[dim] // blocks).reshape((-1,) + (1,) * (len(dims) - dim - 1))

    loudness = one(*shards[0])
    for cut in shards[1:]:
        loudness = loudness * one(*cut)
    return loudness


def picks_of(own_key, rows, number_of, top, lift):
    sequence = jax.random.permutation(jax.random.fold_in(own_key, 1), number_of)
    favour = sequence
    for power in range(3):
        favour = favour * favour // number_of
    favour = favour * lift // number_of
    chance = jax.random.randint(jax.random.fold_in(own_key, 2), (rows, number_of), 0, 4096) + favour
    sure = jax.random.permutation(jax.random.fold_in(own_key, 3), rows)[jnp.arange(number_of) % rows]
    chance = jnp.where(jnp.arange(rows)[:, None] == sure[None, :], 1 << 14, chance)
    merit = chance * number_of + jnp.arange(number_of)
    return lax.top_k(merit.astype(jnp.int32), top)[1].astype(jnp.int32)


def profile(number_of, total, reach, lean):
    loads = [(1 << 20) // math.isqrt(rank ** lean) + 1 for rank in range(2, number_of + 1)]
    surplus, counts = total - reach - (number_of - 1), [1] * (number_of - 1)
    while surplus > 0:
        candidates = [i for i in range(number_of - 1) if counts[i] < reach]
        mass, remaining = sum([loads[i] for i in candidates]), surplus
        for i in candidates:
            extra = min(reach - counts[i], max(1, remaining * loads[i] // mass), surplus)
            counts[i] = counts[i] + extra
            surplus = surplus - extra
    return np.array([reach] + counts)


def ragged_sizes(own_key, count, total, most, skew):
    if count == 2:
        one = jax.random.randint(own_key, (), max(1, total - most), min(most, total - 1) + 1)
        return jnp.stack([one, total - one])
    sizes = jnp.asarray(profile(count, total, most, skew), jnp.int32)
    twos = (count - 1) // 2
    donor, receiver = sizes[1:1 + 2 * twos:2], sizes[2:2 + 2 * twos:2]
    margin = jnp.minimum(donor - 1, most - receiver)
    moved = jax.random.randint(jax.random.fold_in(own_key, 1), (twos,), 0, 1 << 20) % (margin + 1)
    sizes = sizes.at[1:1 + 2 * twos:2].set(donor - moved).at[2:2 + 2 * twos:2].set(receiver + moved)
    return sizes[jax.random.permutation(jax.random.fold_in(own_key, 2), count)]


def scatter_about(stream_key, extent, spread, reach, split=(), held_as=jnp.bfloat16):
    factor_of = block_scale(stream_key, extent, split, -0.22, 0.18) if split else 1.0
    result = jax.random.normal(stream_key, extent, jnp.float32) * spread * factor_of
    return jnp.minimum(jnp.maximum(result, -reach), reach).astype(held_as)


def setup_inputs(seed: int = 0, part: int = 0) -> dict:
    seeds = jax.random.split(jax.random.key(seed), 12)
    part_keys = jax.random.split(jax.random.fold_in(seeds[11], part), 12)
    return {
        "feats": scatter_about(part_keys[0], (CELLS, F), 1.0, 6.0, ((0, 8),)),
        "cell_count": ragged_sizes(part_keys[1], N_DOM, N_DOM * C_DEV * 3 // 4, C_DEV, 2).astype(jnp.int32),
        "tile_col": picks_of(part_keys[2], (CELLS // 128), C_DEV // 128, NB, 0),
        "tile_val": scatter_about(part_keys[3], (CELLS // 128, NB, 128, 128), (NB * 128) ** -0.5, 0.1875, ((0, 8),)),
        "send_list": place_ends(jax.random.randint(part_keys[4], (N_DOM, N_DOM, CAP), 0, C_DEV), jax.random.fold_in(part_keys[4], 1), 0, C_DEV - 1).astype(jnp.int32),
        "send_count": jax.vmap(lambda own: ragged_sizes(own, N_DOM, N_DOM * CAP // 2, CAP, 2))(jax.random.split(part_keys[5], N_DOM)).reshape((N_DOM, N_DOM)).astype(jnp.int32),
        "recv_list": place_ends(jax.random.randint(part_keys[6], (N_DOM, N_DOM, CAP), 0, C_DEV), jax.random.fold_in(part_keys[6], 1), 0, C_DEV - 1).astype(jnp.int32),
        "gate_weight_matrix": scatter_about(seeds[7], (L, F, H), F ** -0.5, 0.375, ((2, 2),)),
        "w_up": scatter_about(seeds[8], (L, F, H), F ** -0.5, 0.375, ((2, 2),)),
        "w_down": scatter_about(seeds[9], (L, H, F), H ** -0.5, 0.25, ((1, 2),)),
        "out_grad": scatter_about(part_keys[10], (CELLS, F), 1.0, 6.0, ((0, 8),)),
    }


def gate_terms(gate_pre):
    sigmoid = jax.nn.sigmoid(gate_pre)
    return gate_pre * sigmoid, sigmoid * (1.0 + gate_pre * (1.0 - sigmoid))


def local_forward(current, tile_col, tile_val):
    block_count = C_DEV // 128
    blocks = current.reshape(N_DOM, block_count, 128, F)
    tiles = tile_val.reshape(N_DOM, block_count, NB, 128, 128)
    columns = tile_col.reshape(N_DOM, block_count, NB)

    def one_part(operands):
        block_rows, partition_tile_rows, part_cols = operands
        picked = block_rows[part_cols]
        summed_messages = jnp.einsum("rjab,rjbf->raf", partition_tile_rows.astype(jnp.float32), picked.astype(jnp.float32))
        return summed_messages.reshape(C_DEV, F)

    return lax.map(one_part, (blocks, tiles, columns))


def local_backward(upstream, tile_col, tile_val):
    block_count = C_DEV // 128
    blocks = upstream.reshape(N_DOM, block_count, 128, F)
    tiles = tile_val.reshape(N_DOM, block_count, NB, 128, 128)
    columns = tile_col.reshape(N_DOM, block_count, NB)

    def one_part(operands):
        block_rows, partition_tile_rows, part_cols = operands
        contribution_part = jnp.einsum("rjab,raf->rjbf", partition_tile_rows.astype(jnp.float32), block_rows.astype(jnp.float32))
        summed_messages = jnp.zeros((block_count, 128, F), jnp.float32).at[part_cols.reshape(-1)].add(
            contribution_part.reshape(block_count * NB, 128, F))
        return summed_messages.reshape(C_DEV, F)

    return lax.map(one_part, (blocks, tiles, columns))


def slot_live(send_count):
    return (jnp.arange(CAP)[None, None, :] < send_count[:, :, None]).astype(jnp.float32)[..., None]


def halo_forward(current, send_list, send_count, recv_list):
    sender = jnp.arange(N_DOM)[:, None, None]
    leaving = current[sender, send_list].astype(jnp.float32) * slot_live(send_count)
    arriving = jnp.swapaxes(leaving, 0, 1)
    flat_target = (sender * C_DEV + recv_list).astype(jnp.int32).reshape(-1)
    summed_messages = jnp.zeros((N_DOM * C_DEV, F), jnp.float32).at[flat_target].add(arriving.reshape(-1, F))
    return summed_messages.reshape(N_DOM, C_DEV, F)


def halo_backward(upstream, send_list, send_count, recv_list):
    owner = jnp.arange(N_DOM)[:, None, None]
    flat_target = (owner * C_DEV + recv_list).astype(jnp.int32).reshape(-1)
    picked = upstream.reshape(N_DOM * C_DEV, F)[flat_target].reshape(N_DOM, N_DOM, CAP, F).astype(jnp.float32)
    returning = jnp.swapaxes(picked, 0, 1) * slot_live(send_count)
    flat_source = (owner * C_DEV + send_list).astype(jnp.int32).reshape(-1)
    summed_messages = jnp.zeros((N_DOM * C_DEV, F), jnp.float32).at[flat_source].add(returning.reshape(-1, F))
    return summed_messages.reshape(N_DOM, C_DEV, F)


def reference(feats, cell_count, tile_col, tile_val, send_list, send_count, recv_list, gate_weight_matrix, w_up, w_down, out_grad):
    live_mask = (jnp.arange(C_DEV)[None, :] < cell_count[:, None]).astype(jnp.float32)[..., None]
    current = (feats.reshape(N_DOM, C_DEV, F).astype(jnp.float32) * live_mask).astype(jnp.bfloat16)
    stored = []
    for layer_index in range(L):
        summed_messages = local_forward(current, tile_col, tile_val) + halo_forward(current, send_list, send_count, recv_list)
        acts = summed_messages.astype(jnp.bfloat16).reshape(CELLS, F)
        gate_pre = jnp.dot(acts, gate_weight_matrix[layer_index], preferred_element_type=jnp.float32)
        up_preactivation = jnp.dot(acts, w_up[layer_index], preferred_element_type=jnp.float32)
        silu_value, silu_slope = gate_terms(gate_pre)
        hidden = (silu_value * up_preactivation).astype(jnp.bfloat16)
        mixed = jnp.dot(hidden, w_down[layer_index], preferred_element_type=jnp.float32).reshape(N_DOM, C_DEV, F)
        stored.append((acts, up_preactivation, silu_value, silu_slope, hidden))
        current = ((current.astype(jnp.float32) + mixed) * live_mask).astype(jnp.bfloat16)
    final = current.reshape(CELLS, F)
    carried = out_grad.reshape(N_DOM, C_DEV, F).astype(jnp.float32)
    grad_gates, up_weight_gradients, grad_downs = [], [], []
    for layer_index in reversed(range(L)):
        acts, up_preactivation, silu_value, silu_slope, hidden = stored[layer_index]
        upstream = carried * live_mask
        down_in = upstream.astype(jnp.bfloat16).reshape(CELLS, F)
        grad_downs.append(jnp.dot(hidden.T, down_in, preferred_element_type=jnp.float32))
        hidden_grad = jnp.dot(down_in, w_down[layer_index].T, preferred_element_type=jnp.float32)
        gate_grad = (hidden_grad * up_preactivation * silu_slope).astype(jnp.bfloat16)
        up_grad = (hidden_grad * silu_value).astype(jnp.bfloat16)
        grad_gates.append(jnp.dot(acts.T, gate_grad, preferred_element_type=jnp.float32))
        up_weight_gradients.append(jnp.dot(acts.T, up_grad, preferred_element_type=jnp.float32))
        agg_grad = (jnp.dot(gate_grad, gate_weight_matrix[layer_index].T, preferred_element_type=jnp.float32)
                    + jnp.dot(up_grad, w_up[layer_index].T, preferred_element_type=jnp.float32)).astype(jnp.bfloat16)
        agg_grad = agg_grad.reshape(N_DOM, C_DEV, F)
        carried = upstream + local_backward(agg_grad, tile_col, tile_val) + halo_backward(
            agg_grad, send_list, send_count, recv_list)
    feat_grad = (carried * live_mask).reshape(CELLS, F)
    grad_gate = jnp.stack(grad_gates[::-1])
    grad_up = jnp.stack(up_weight_gradients[::-1])
    down_weight_gradient = jnp.stack(grad_downs[::-1])
    return (final, feat_grad, grad_gate, grad_up, down_weight_gradient)
```

```python
import functools

import jax
import jax.numpy as jnp
from jax import lax
from jax.experimental import pallas as pl
from jax.experimental.pallas import tpu as pltpu
from jax.sharding import PartitionSpec as P

BF16 = jnp.bfloat16
F32 = jnp.float32
LANES = 128
BLOCK = 128
VMEM = pl.BlockSpec(memory_space=pltpu.VMEM)
SMEM = pl.BlockSpec(memory_space=pltpu.SMEM)
GRANT = 40 * 1024 * 1024


def call(kernel, outs, ins, flops, name, scratch=(), smem=0):
    moved = sum(x.size * x.dtype.itemsize for x in (*ins, *outs))
    return pl.pallas_call(
        kernel,
        out_shape=outs,
        in_specs=[SMEM] * smem + [VMEM] * (len(ins) - smem),
        out_specs=[VMEM] * len(outs),
        scratch_shapes=list(scratch),
        cost_estimate=pl.CostEstimate(flops=flops, bytes_accessed=moved, transcendentals=0),
        compiler_params=pltpu.CompilerParams(vmem_limit_bytes=GRANT),
        name=name,
    )(*ins)


def shape(dims, dtype):
    return jax.ShapeDtypeStruct(tuple(dims), dtype)


def chunk_of(rows):
    for size in (256, 128):
        if rows % size == 0:
            return size
    return rows


def mm(a, b):
    return jnp.dot(a, b, preferred_element_type=F32)


def mm_t(a, b):
    return lax.dot_general(a, b, (((1,), (1,)), ((), ())), preferred_element_type=F32)


def mm_rows(a, b):
    return lax.dot_general(a, b, (((0,), (0,)), ((), ())), preferred_element_type=F32)


def window(i, size):
    return pl.ds(pl.multiple_of(i * size, size), size)


def live(count_ref, start, rows, width):
    index = lax.broadcasted_iota(jnp.int32, (rows, width), 0) + start
    return index < count_ref[0]


def gather_rows(col_ref, source, out_ref):
    slots, rows = out_ref.shape[0], source.shape[0]
    size = chunk_of(slots)
    lanes = lax.broadcasted_iota(jnp.int32, (size, LANES), 1)

    def step(i, carry):
        at = window(i, size)
        col = col_ref[at, :]
        pick = jnp.concatenate(
            [jnp.where(col == lanes + first, 1.0, 0.0).astype(BF16) for first in range(0, rows, LANES)],
            axis=1,
        )
        out_ref[at, :] = mm(pick, source[...]).astype(BF16)
        return carry

    lax.fori_loop(0, slots // size, step, 0)


def scatter_rows(row_ref, start, rows, arriving):
    slots = row_ref.shape[1]
    index = lax.broadcasted_iota(jnp.int32, (rows, slots), 0) + start
    pick = jnp.where(row_ref[0:1, :] == index, 1.0, 0.0).astype(BF16)
    return mm(pick, arriving[...])


def send_kernel(col_ref, feats_ref, out_ref):
    gather_rows(col_ref, feats_ref, out_ref)


def first_local_kernel(count_ref, cols_ref, feats_ref, tile_ref, state_ref, dense_ref, flip_ref, sum_ref):
    rows = feats_ref.shape[0]
    row_blocks, per_row = cols_ref.shape
    state_ref[...] = jnp.where(live(count_ref, 0, rows, feats_ref.shape[1]), feats_ref[...], jnp.zeros((), BF16))
    dense_ref[...] = jnp.zeros_like(dense_ref)
    flip_ref[...] = jnp.zeros_like(flip_ref)

    for r in range(row_blocks):
        for j in range(per_row):
            at = pl.ds(pl.multiple_of(cols_ref[r, j] * BLOCK, BLOCK), BLOCK)
            tile = tile_ref[r, j]
            dense_ref[r * BLOCK : (r + 1) * BLOCK, at] = tile
            flip_ref[at, r * BLOCK : (r + 1) * BLOCK] = tile.T
    dense_sum(dense_ref, state_ref, sum_ref)


def dense_sum(dense_ref, state_ref, sum_ref, extra=None):
    size = chunk_of(sum_ref.shape[0])

    def step(i, carry):
        at = window(i, size)
        total = mm(dense_ref[at, :], state_ref[...])
        sum_ref[at, :] = total if extra is None else total + extra(at, i * size)
        return carry

    lax.fori_loop(0, sum_ref.shape[0] // size, step, 0)


def local_kernel(dense_ref, state_ref, sum_ref):
    dense_sum(dense_ref, state_ref, sum_ref)


def gates(acts, weights):
    result = []
    for gate_ref, up_ref, _ in weights:
        gate = mm(acts, gate_ref[...])
        up = mm(acts, up_ref[...])
        sig = 0.5 * jnp.tanh(0.5 * gate) + 0.5
        result.append((gate, up, sig, gate * sig))
    return result


def grads_into(at, acts, terms, down_in, weights, gate_out, up_out, agg_out):
    agg = None
    for half, ((gate, up, sig, silu), (gate_ref, up_ref, down_ref)) in enumerate(zip(terms, weights)):
        hidden_grad = mm_t(down_in, down_ref[...])
        slope = sig * (1.0 + gate * (1.0 - sig))
        gate_grad = (hidden_grad * up * slope).astype(BF16)
        up_grad = (hidden_grad * silu).astype(BF16)
        part = mm_t(gate_grad, gate_ref[...]) + mm_t(up_grad, up_ref[...])
        agg = part if agg is None else agg + part
        if half == 0:
            gate_out[at, :] = gate_grad
            up_out[at, :] = up_grad
    agg_out[at, :] = agg.astype(BF16)


def triples(refs):
    return [tuple(refs[i : i + 3]) for i in range(0, len(refs), 3)]


def forward_kernel(parts, count_ref, col_ref, row_ref, sum_ref, arriving_ref, state_ref, *refs):
    weights = triples(refs[: 3 * parts])
    acts_ref, next_ref, out_ref = refs[3 * parts :]
    rows, width = state_ref.shape
    size = chunk_of(rows)

    def step(i, carry):
        at = window(i, size)
        acts = (sum_ref[at, :] + scatter_rows(row_ref, i * size, size, arriving_ref)).astype(BF16)
        acts_ref[at, :] = acts
        mixed = None
        for (gate, up, sig, silu), (_, _, down_ref) in zip(gates(acts, weights), weights):
            part = mm((silu * up).astype(BF16), down_ref[...])
            mixed = part if mixed is None else mixed + part
        total = state_ref[at, :].astype(F32) + mixed
        next_ref[at, :] = jnp.where(live(count_ref, i * size, size, width), total, 0.0).astype(BF16)
        return carry

    lax.fori_loop(0, rows // size, step, 0)
    gather_rows(col_ref, next_ref, out_ref)


def turn_kernel(parts, count_ref, col_ref, row_ref, sum_ref, arriving_ref, state_ref, grad_ref, *refs):
    weights = triples(refs[: 3 * parts])
    acts_ref, final_ref, hidden_ref, gate_out, up_out, agg_ref, out_ref = refs[3 * parts :]
    rows, width = state_ref.shape
    size = chunk_of(rows)

    def step(i, carry):
        at = window(i, size)
        acts = (sum_ref[at, :] + scatter_rows(row_ref, i * size, size, arriving_ref)).astype(BF16)
        acts_ref[at, :] = acts
        terms = gates(acts, weights)
        mixed = None
        for half, ((gate, up, sig, silu), (_, _, down_ref)) in enumerate(zip(terms, weights)):
            hidden = (silu * up).astype(BF16)
            if half == 0:
                hidden_ref[at, :] = hidden
            part = mm(hidden, down_ref[...])
            mixed = part if mixed is None else mixed + part
        total = state_ref[at, :].astype(F32) + mixed
        alive = live(count_ref, i * size, size, width)
        final_ref[at, :] = jnp.where(alive, total, 0.0).astype(BF16)
        down_in = jnp.where(alive, grad_ref[at, :], jnp.zeros((), BF16))
        grads_into(at, acts, terms, down_in, weights, gate_out, up_out, agg_ref)
        return carry

    lax.fori_loop(0, rows // size, step, 0)
    gather_rows(col_ref, agg_ref, out_ref)


def backward_kernel(parts, count_ref, col_ref, row_ref, sum_ref, arriving_ref, acts_ref, *refs):
    weights = triples(refs[: 3 * parts])
    upstream_ref, down_in_ref, hidden_ref, gate_out, up_out, agg_ref, out_ref = refs[3 * parts :]
    rows, width = acts_ref.shape
    size = chunk_of(rows)

    def step(i, carry):
        at = window(i, size)
        carried = sum_ref[at, :] + scatter_rows(row_ref, i * size, size, arriving_ref)
        upstream = jnp.where(live(count_ref, i * size, size, width), carried, 0.0)
        upstream_ref[at, :] = upstream
        down_in = upstream.astype(BF16)
        down_in_ref[at, :] = down_in
        acts = acts_ref[at, :]
        terms = gates(acts, weights)
        hidden_ref[at, :] = (terms[0][3] * terms[0][1]).astype(BF16)
        grads_into(at, acts, terms, down_in, weights, gate_out, up_out, agg_ref)
        return carry

    lax.fori_loop(0, rows // size, step, 0)
    gather_rows(col_ref, agg_ref, out_ref)


def cover_kernel(count_ref, flip_ref, agg_ref, up_ref, acts_ref, hidden_ref, gate_ref, upg_ref, down_ref, sum_ref, dw_ref):
    width = agg_ref.shape[1]
    size = chunk_of(sum_ref.shape[0])

    def extra(at, start):
        return jnp.where(live(count_ref, start, size, width), up_ref[at, :].astype(F32), 0.0)

    dense_sum(flip_ref, agg_ref, sum_ref, extra)
    down_in = down_ref[...]
    rows = down_in.shape[0]
    down_in = jnp.where(live(count_ref, 0, rows, down_in.shape[1]), down_in, jnp.zeros((), BF16))
    dw_ref[0] = mm_rows(acts_ref[...], gate_ref[...]).astype(BF16)
    dw_ref[1] = mm_rows(acts_ref[...], upg_ref[...]).astype(BF16)
    dw_ref[2] = mm_rows(hidden_ref[...], down_in).astype(BF16)


def last_kernel(count_ref, row_ref, sum_ref, arriving_ref, out_ref):
    rows, width = out_ref.shape
    size = chunk_of(rows)

    def step(i, carry):
        at = window(i, size)
        carried = sum_ref[at, :] + scatter_rows(row_ref, i * size, size, arriving_ref)
        out_ref[at, :] = jnp.where(live(count_ref, i * size, size, width), carried, 0.0)
        return carry

    lax.fori_loop(0, rows // size, step, 0)


def local(
    feats,
    cell_count,
    tile_col,
    tile_val,
    send_list,
    send_count,
    recv_list,
    gate_weight_matrix,
    w_up,
    w_down,
    out_grad,
):
    rows, width = feats.shape
    peers, slot_count = send_list.shape[1:]
    slots = peers * slot_count
    layers = gate_weight_matrix.shape[0]
    parts = lax.axis_size("mp")

    in_use = jnp.arange(slot_count)[None, :] < send_count[0][:, None]
    sources = jnp.where(in_use & (send_list[0] < cell_count[0]), send_list[0], -1).reshape(-1)
    targets = recv_list[0].reshape(-1)
    send_col, recv_col = (jnp.broadcast_to(x[:, None], (slots, LANES)) for x in (sources, targets))
    send_row, recv_row = (x[None, :] for x in (sources, targets))

    def exchange(sent):
        moved = lax.all_to_all(
            sent.reshape(peers, slot_count, width), "dom", split_axis=0, concat_axis=0, tiled=True
        )
        return moved.reshape(slots, width)

    turns = [[(d, (d + t) % parts) for d in range(parts)] for t in range(1, parts)]
    mine = (gate_weight_matrix, w_up, w_down)
    held = [mine] + [tuple(lax.ppermute(w, "mp", turn) for w in mine) for turn in turns]

    def weights(layer):
        return [w[layer] for trio in held for w in trio]

    hidden_width = gate_weight_matrix.shape[2]
    state_shape, sum_shape, slot_shape = (
        shape((rows, width), BF16),
        shape((rows, width), F32),
        shape((slots, width), BF16),
    )
    half_shape = shape((rows, hidden_width), BF16)
    square = shape((rows, rows), BF16)
    local_flops = 2 * rows * rows * width
    slot_flops = 2 * rows * slots * width
    layer_flops = 6 * rows * width * hidden_width * parts

    (outgoing,) = call(send_kernel, [slot_shape], [send_col, feats], slot_flops, "send")
    arriving = exchange(outgoing)
    state, dense, flip, total = call(
        first_local_kernel,
        [state_shape, square, square, sum_shape],
        [cell_count, tile_col, feats, tile_val],
        local_flops,
        "first_local",
        smem=2,
    )
    kept = []
    for layer in range(layers - 1):
        acts, state, outgoing = call(
            functools.partial(forward_kernel, parts),
            [state_shape, state_shape, slot_shape],
            [cell_count, send_col, recv_row, total, arriving, state, *weights(layer)],
            layer_flops + 2 * slot_flops,
            "forward",
            smem=1,
        )
        kept.append(acts)
        arriving = exchange(outgoing)
        (total,) = call(local_kernel, [sum_shape], [dense, state], local_flops, "local")
    acts, final, hidden, gate_grad, up_grad, agg, outgoing = call(
        functools.partial(turn_kernel, parts),
        [state_shape, state_shape, half_shape, half_shape, half_shape, state_shape, slot_shape],
        [cell_count, recv_col, recv_row, total, arriving, state, out_grad, *weights(layers - 1)],
        3 * layer_flops + 2 * slot_flops,
        "turn",
        smem=1,
    )
    upstream, down_in = out_grad, out_grad
    grads = []
    for layer in reversed(range(layers)):
        arriving = exchange(outgoing)
        total, weight_grads = call(
            cover_kernel,
            [sum_shape, shape((3, width, hidden_width), BF16)],
            [cell_count, flip, agg, upstream, acts, hidden, gate_grad, up_grad, down_in],
            local_flops + layer_flops // parts,
            "cover",
            smem=1,
        )
        grads.append(weight_grads)
        if layer == 0:
            break
        acts = kept[layer - 1]
        upstream, down_in, hidden, gate_grad, up_grad, agg, outgoing = call(
            functools.partial(backward_kernel, parts),
            [sum_shape, state_shape, half_shape, half_shape, half_shape, state_shape, slot_shape],
            [cell_count, recv_col, send_row, total, arriving, acts, *weights(layer - 1)],
            3 * layer_flops + 2 * slot_flops,
            "backward",
            smem=1,
        )
    (feat_grad,) = call(
        last_kernel,
        [sum_shape],
        [cell_count, send_row, total, arriving],
        slot_flops,
        "last",
        smem=1,
    )
    summed = jnp.stack(grads[::-1], axis=1)
    chunks = summed.reshape(peers, -1, width)
    parts_in = lax.all_to_all(chunks, "dom", split_axis=0, concat_axis=0, tiled=True)
    own = jnp.sum(parts_in.astype(F32), axis=0).astype(BF16)
    full = lax.all_to_all(
        jnp.broadcast_to(own[None], (peers, *own.shape)), "dom", split_axis=0, concat_axis=0, tiled=True
    )
    full = full.reshape(3, layers, width, hidden_width).astype(F32)
    return (final, feat_grad, full[0], full[1], full[2])


def solution(mesh):
    return jax.shard_map(
        local,
        mesh=mesh,
        in_specs=(
            P(("groups", "dom"), None),
            P(("groups", "dom")),
            P(("groups", "dom"), None),
            P(("groups", "dom"), None, None, None),
            P(("groups", "dom"), None, None),
            P(("groups", "dom"), None),
            P(("groups", "dom"), None, None),
            P(None, None, "mp"),
            P(None, None, "mp"),
            P(None, "mp", None),
            P(("groups", "dom"), None),
        ),
        out_specs=(
            P(("groups", "dom"), None),
            P(("groups", "dom"), None),
            P("groups", None, "mp"),
            P("groups", None, "mp"),
            P("groups", "mp", None),
        ),
        check_vma=False,
    )
```

```python
import functools

import jax
import jax.numpy as jnp
from jax import lax
from jax.experimental import pallas as pl
from jax.experimental.pallas import tpu as pltpu
from jax.sharding import PartitionSpec as P

BF16 = jnp.bfloat16
F32 = jnp.float32
LANES = 128
BLOCK = 128
SMEM = pl.BlockSpec(memory_space=pltpu.SMEM)
CHUNK = 1536
SUB = 512
SLOTS = 512


def shape(dims, dtype):
    return jax.ShapeDtypeStruct(tuple(dims), dtype)


def part(ref, cut, c):
    if cut == "whole":
        return ref
    if cut == "rows":
        return ref.at[pl.ds(c * CHUNK, CHUNK)]
    if cut == "columns":
        return ref.at[:, pl.ds(c * CHUNK, CHUNK)]
    return ref.at[pl.ds(c * cut, cut)]


class Layer:
    def __init__(self, index):
        self.index = index


class Traffic:
    def __init__(self, steps, ins, outs, in_sems, out_sems):
        self.steps, self.ins, self.outs, self.in_sems, self.out_sems = steps, ins, outs, in_sems, out_sems
        self.leaving = []
        for c in range(steps):
            for k in range(len(ins)):
                if self.has(k, c):
                    self.arriving(k, c).start()

    def has(self, k, c):
        cut = self.ins[k][2]
        return cut not in ("near", "later") and (c == 0 or not (cut == "whole" or isinstance(cut, Layer)))

    def arriving(self, k, c):
        far, near, cut = self.ins[k]
        if isinstance(cut, Layer):
            return pltpu.make_async_copy(far.at[cut.index], near, self.in_sems.at[k, 0])
        return pltpu.make_async_copy(part(far, cut, c), part(near, cut, c), self.in_sems.at[k, c])

    def need(self, c, *which):
        for k in which or range(len(self.ins)):
            if self.has(k, c):
                self.arriving(k, c).wait()

    def put(self, k, c=0):
        near, far, cut = self.outs[k]
        copy = pltpu.make_async_copy(part(near, cut, c), part(far, cut, c), self.out_sems.at[k, c])
        copy.start()
        self.leaving.append(copy)

    def finish(self):
        for copy in self.leaving:
            copy.wait()


def call(kernel, steps, outs, ins, flops, name, scratch=()):
    moved = sum(x.size * x.dtype.itemsize for x, _ in (*ins, *outs))
    far_ins = [(x, cut) for x, cut in ins if cut is not None]
    scalars = len(ins) - len(far_ins)
    kept_outs = [k for k, (_, cut) in enumerate(outs) if cut != "later"]
    staged = [k for k, (_, cut) in enumerate(far_ins) if cut not in ("near", "later")]

    def body(*refs):
        fixed = refs[:scalars]
        far_in = refs[scalars : len(ins)]
        far_out = refs[len(ins) : len(ins) + len(outs)]
        rest = refs[len(ins) + len(outs) :]
        near_in = list(far_in)
        for slot, k in enumerate(staged):
            near_in[k] = rest[slot]
        rest = rest[len(staged) :]
        near_out, rest = rest[: len(kept_outs)], rest[len(kept_outs) :]
        near_out = [near_out[kept_outs.index(k)] if k in kept_outs else None for k in range(len(outs))]
        (in_sems, out_sems), own = rest[:2], rest[2:]
        traffic = Traffic(
            steps,
            [(f, n, cut) for f, n, (_, cut) in zip(far_in, near_in, far_ins)],
            [(n, f, cut) for n, f, (_, cut) in zip(near_out, far_out, outs)],
            in_sems,
            out_sems,
        )
        kernel(traffic, *fixed, *near_in, *(near_out[k] for k in kept_outs), *own)
        traffic.finish()

    def held(x, cut):
        return pltpu.VMEM(x.shape[1:] if isinstance(cut, Layer) else x.shape, x.dtype)

    spaces = [pltpu.VMEM if cut == "near" else pl.ANY for _, cut in far_ins]
    return pl.pallas_call(
        body,
        out_shape=[x for x, _ in outs],
        in_specs=[SMEM] * scalars + [pl.BlockSpec(memory_space=space) for space in spaces],
        out_specs=[pl.BlockSpec(memory_space=pl.ANY)] * len(outs),
        scratch_shapes=[
            *(held(*far_ins[k]) for k in staged),
            *(pltpu.VMEM(outs[k][0].shape, outs[k][0].dtype) for k in kept_outs),
            pltpu.SemaphoreType.DMA((len(far_ins), steps)),
            pltpu.SemaphoreType.DMA((len(outs), steps)),
            *scratch,
        ],
        cost_estimate=pl.CostEstimate(flops=flops, bytes_accessed=moved, transcendentals=0),
        name=name,
    )(*[x for x, _ in ins])


def rows_of(c):
    return slice(c * CHUNK, (c + 1) * CHUNK)


def inner(c):
    return range(c * CHUNK, (c + 1) * CHUNK, SUB)


def mm(a, b):
    return jnp.dot(a, b, preferred_element_type=F32)


def mm_t(a, b):
    return lax.dot_general(a, b, (((1,), (1,)), ((), ())), preferred_element_type=F32)


def mm_rows(a, b):
    return lax.dot_general(a, b, (((0,), (0,)), ((), ())), preferred_element_type=F32)


def live(count_ref, start, rows, width):
    index = lax.broadcasted_iota(jnp.int32, (rows, width), 0) + start
    return index < count_ref[0]


def fill_columns(col_ref, list_ref, used):
    peers, n = list_ref.shape[1:]
    down = lax.broadcasted_iota(jnp.int32, (n, n), 0)
    across = lax.broadcasted_iota(jnp.int32, (n, n), 1)

    def step(q, carry):
        line = jnp.broadcast_to(list_ref[0, pl.ds(q, 1), :], (n, n))
        kept = (down == across) & used(q, across, line)
        col = jnp.sum(jnp.where(kept, line + 1, 0), axis=1, keepdims=True) - 1
        col_ref[pl.ds(pl.multiple_of(q * n, n), n), :] = jnp.broadcast_to(col, (n, LANES))
        return carry

    lax.fori_loop(0, peers, step, 0, unroll=4)


def fill_row(row_ref, list_ref, used):
    peers, n = list_ref.shape[1:]
    across = lax.broadcasted_iota(jnp.int32, (1, n), 1)
    for q in range(peers):
        line = list_ref[0, q : q + 1, :]
        row_ref[0:1, q * n : (q + 1) * n] = jnp.where(used(q, across, line), line, -1)


def sent(count_ref, used_ref):
    return lambda q, k, row: (k < used_ref[0, q]) & (row < count_ref[0])


def always(q, k, row):
    return row >= 0


def gather_rows(col_ref, source_ref, out_ref):
    slots, rows = out_ref.shape[0], source_ref.shape[0]
    lanes = lax.broadcasted_iota(jnp.int32, (SLOTS, LANES), 1)

    def step(i, carry):
        at = pl.ds(pl.multiple_of(i * SLOTS, SLOTS), SLOTS)
        col = col_ref[at, :]
        pick = jnp.concatenate(
            [jnp.where(col == lanes + first, 1.0, 0.0).astype(BF16) for first in range(0, rows, LANES)], axis=1
        )
        out_ref[at, :] = mm(pick, source_ref[...]).astype(BF16)
        return carry

    lax.fori_loop(0, slots // SLOTS, step, 0)


def scatter_rows(row_ref, start, rows, arriving):
    slots = row_ref.shape[1]
    index = lax.broadcasted_iota(jnp.int32, (rows, slots), 0) + start
    pick = jnp.where(row_ref[0:1, :] == index, 1.0, 0.0).astype(BF16)
    return mm(pick, arriving[...])


def send_kernel(traffic, count_ref, used_ref, list_ref, feats_ref, out_ref, col_ref):
    traffic.need(0)
    fill_columns(col_ref, list_ref, sent(count_ref, used_ref))
    traffic.put(1)
    for c in range(1, traffic.steps):
        traffic.need(c)
    gather_rows(col_ref, feats_ref, out_ref)
    traffic.put(0)


class Dense:
    def __init__(self, cols_ref, tile_ref, dense_ref, sems):
        self.tile_ref, self.dense_ref, self.sems = tile_ref, dense_ref, sems
        self.row_blocks, self.per_row = tile_ref.shape[:2]
        self.cols_ref = cols_ref
        for r in range(self.row_blocks):
            for j in range(self.per_row):
                self.copy(r, j).start()

    def copy(self, r, j):
        at = pl.ds(pl.multiple_of(self.cols_ref[r, j] * BLOCK, BLOCK), BLOCK)
        return pltpu.make_async_copy(
            self.tile_ref.at[r, j], self.dense_ref.at[pl.ds(r * BLOCK, BLOCK), at], self.sems.at[r]
        )

    def zero_others(self, rest_ref):
        columns = self.dense_ref.shape[1] // BLOCK
        for r in range(self.row_blocks):
            named = 0
            for j in range(self.per_row):
                named = named | (1 << self.cols_ref[r, j])
            count = 0
            for c in range(columns):
                rest_ref[count] = c
                count = count + 1 - ((named >> c) & 1)
            for k in range(columns - self.per_row):
                at = pl.ds(pl.multiple_of(rest_ref[k] * BLOCK, BLOCK), BLOCK)
                self.dense_ref[r * BLOCK : (r + 1) * BLOCK, at] = jnp.zeros((BLOCK, BLOCK), BF16)

    def need(self, r):
        for j in range(self.per_row):
            self.copy(r, j).wait()


def first_local_kernel(
    traffic, count_ref, used_ref, cols_ref, send_ref, recv_ref, feats_ref, tile_ref,
    state_ref, sum_ref, send_row_ref, recv_row_ref, recv_col_ref, dense_ref, rest_ref, sems,
):
    dense = Dense(cols_ref, tile_ref, dense_ref, sems)
    dense.zero_others(rest_ref)
    rows, width = feats_ref.shape
    traffic.need(0)
    fill_row(send_row_ref, send_ref, sent(count_ref, used_ref))
    fill_row(recv_row_ref, recv_ref, always)
    fill_columns(recv_col_ref, recv_ref, always)
    state_ref[...] = jnp.where(live(count_ref, 0, rows, width), feats_ref[...], jnp.zeros((), BF16))
    for k in (0, 2, 3, 4):
        traffic.put(k)
    local_sums(traffic, dense, dense_ref, state_ref, sum_ref, 1)


def local_sums(traffic, dense, dense_ref, state_ref, sum_ref, out):
    for c in range(traffic.steps):
        for r in range(c * CHUNK // BLOCK, (c + 1) * CHUNK // BLOCK):
            dense.need(r)
        sum_ref[rows_of(c), :] = mm(dense_ref[rows_of(c), :], state_ref[...])
        traffic.put(out, c)


def local_kernel(traffic, cols_ref, state_ref, tile_ref, sum_ref, dense_ref, rest_ref, sems):
    dense = Dense(cols_ref, tile_ref, dense_ref, sems)
    dense.zero_others(rest_ref)
    traffic.need(0)
    local_sums(traffic, dense, dense_ref, state_ref, sum_ref, 0)


def turned_local_kernel(traffic, count_ref, cols_ref, agg_ref, up_ref, tile_ref, sum_ref, dense_ref, rest_ref, sems):
    dense = Dense(cols_ref, tile_ref, dense_ref, sems)
    dense.zero_others(rest_ref)
    width = agg_ref.shape[1]
    traffic.need(0)
    for r in range(dense.row_blocks):
        dense.need(r)
    for c in range(traffic.steps):
        if c > 0:
            traffic.need(c)
        at = rows_of(c)
        upstream = jnp.where(live(count_ref, c * CHUNK, CHUNK, width), up_ref[at, :].astype(F32), 0.0)
        sum_ref[at, :] = mm_rows(dense_ref[:, at], agg_ref[...]) + upstream
        traffic.put(0, c)


def triples(refs):
    return [tuple(refs[i : i + 3]) for i in range(0, len(refs), 3)]


def gates(acts, weights):
    result = []
    for gate_ref, up_ref, _ in weights:
        gate = mm(acts, gate_ref[...])
        up = mm(acts, up_ref[...])
        sig = 0.5 * jnp.tanh(0.5 * gate) + 0.5
        result.append((gate, up, sig, gate * sig))
    return result


def layer_grads(at, acts, terms, down_in, weights, agg_ref, kept):
    agg = None
    for part, ((gate, up, sig, silu), (gate_ref, up_ref, down_ref)) in enumerate(zip(terms, weights)):
        hidden_grad = mm_t(down_in, down_ref[...])
        slope = sig * (1.0 + gate * (1.0 - sig))
        gate_grad = (hidden_grad * up * slope).astype(BF16)
        up_grad = (hidden_grad * silu).astype(BF16)
        more = mm_t(gate_grad, gate_ref[...]) + mm_t(up_grad, up_ref[...])
        agg = more if agg is None else agg + more
        if part == 0:
            for ref, value in zip(kept, ((silu * up).astype(BF16), gate_grad, up_grad, down_in)):
                ref[at, :] = value
    agg_ref[at, :] = agg.astype(BF16)


def weight_grads(acts_ref, kept, dw_ref):
    hidden_ref, gate_ref, up_ref, down_ref = kept
    pairs = ((acts_ref, gate_ref), (acts_ref, up_ref), (hidden_ref, down_ref))
    for k, (left_ref, right_ref) in enumerate(pairs):
        size = left_ref.shape[1]
        dw_ref[k * size : (k + 1) * size, :] = mm_rows(left_ref[...], right_ref[...]).astype(BF16)


def mix(terms, weights):
    mixed = None
    for (gate, up, sig, silu), (_, _, down_ref) in zip(terms, weights):
        part = mm((silu * up).astype(BF16), down_ref[...])
        mixed = part if mixed is None else mixed + part
    return mixed


def forward_kernel(parts, traffic, count_ref, col_ref, row_ref, arriving_ref, *refs):
    weights = triples(refs[: 3 * parts])
    sum_ref, state_ref, acts_ref, next_ref, out_ref = refs[3 * parts :]
    width = state_ref.shape[1]
    for c in range(traffic.steps):
        traffic.need(c, *range(1, len(traffic.ins)))
        for first in inner(c):
            at = slice(first, first + SUB)
            acts = (sum_ref[at, :] + scatter_rows(row_ref, first, SUB, arriving_ref)).astype(BF16)
            acts_ref[at, :] = acts
            after = state_ref[at, :].astype(F32) + mix(gates(acts, weights), weights)
            next_ref[at, :] = jnp.where(live(count_ref, first, SUB, width), after, 0.0).astype(BF16)
        traffic.put(0, c)
        traffic.put(1, c)
    traffic.need(0, 0)
    gather_rows(col_ref, next_ref, out_ref)
    traffic.put(2)


def turn_kernel(parts, traffic, count_ref, col_ref, row_ref, arriving_ref, *refs):
    weights = triples(refs[: 3 * parts])
    sum_ref, state_ref, grad_ref, final_ref, agg_ref, out_ref, dw_ref, acts_ref, *kept = refs[3 * parts :]
    width = state_ref.shape[1]
    for c in range(traffic.steps):
        traffic.need(c, *range(1, len(traffic.ins)))
        for first in inner(c):
            at = slice(first, first + SUB)
            acts = (sum_ref[at, :] + scatter_rows(row_ref, first, SUB, arriving_ref)).astype(BF16)
            acts_ref[at, :] = acts
            terms = gates(acts, weights)
            after = state_ref[at, :].astype(F32) + mix(terms, weights)
            alive = live(count_ref, first, SUB, width)
            final_ref[at, :] = jnp.where(alive, after, 0.0).astype(BF16)
            down_in = jnp.where(alive, grad_ref[at, :], jnp.zeros((), BF16))
            layer_grads(at, acts, terms, down_in, weights, agg_ref, kept)
        traffic.put(0, c)
        traffic.put(1, c)
    traffic.need(0, 0)
    gather_rows(col_ref, agg_ref, out_ref)
    traffic.put(2)
    weight_grads(acts_ref, kept, dw_ref)
    traffic.put(3)


def put_pieces(traffic, k, sources, sem):
    far = traffic.outs[k][1]
    for q in range(far.shape[0]):
        first = 0
        for source in sources:
            rows = source.shape[0] // far.shape[0]
            copy = pltpu.make_async_copy(
                source.at[pl.ds(q * rows, rows)], far.at[q, pl.ds(first, rows)], sem.at[q]
            )
            copy.start()
            traffic.leaving.append(copy)
            first += rows


def backward_kernel(parts, traffic, count_ref, col_ref, row_ref, arriving_ref, *refs):
    weights = triples(refs[: 3 * parts])
    sum_ref, acts_ref, upstream_ref, agg_ref, out_ref, dw_ref, sem, *kept = refs[3 * parts :]
    width = acts_ref.shape[1]
    for c in range(traffic.steps):
        traffic.need(c, *range(1, len(traffic.ins)))
        for first in inner(c):
            at = slice(first, first + SUB)
            carried = sum_ref[at, :] + scatter_rows(row_ref, first, SUB, arriving_ref)
            upstream = jnp.where(live(count_ref, first, SUB, width), carried, 0.0)
            upstream_ref[at, :] = upstream
            acts = acts_ref[at, :]
            layer_grads(at, acts, gates(acts, weights), upstream.astype(BF16), weights, agg_ref, kept)
        traffic.put(0, c)
        traffic.put(1, c)
    traffic.need(0, 0)
    gather_rows(col_ref, agg_ref, out_ref)
    weight_grads(acts_ref, kept, dw_ref)
    put_pieces(traffic, 2, (out_ref, dw_ref), sem)


def last_kernel(traffic, count_ref, row_ref, arriving_ref, sum_ref, out_ref):
    width = out_ref.shape[1]
    for c in range(traffic.steps):
        traffic.need(c)
        for first in inner(c):
            at = slice(first, first + SUB)
            carried = sum_ref[at, :] + scatter_rows(row_ref, first, SUB, arriving_ref)
            out_ref[at, :] = jnp.where(live(count_ref, first, SUB, width), carried, 0.0)
        traffic.put(0, c)


def local(
    feats,
    cell_count,
    tile_col,
    tile_val,
    send_list,
    send_count,
    recv_list,
    gate_weight_matrix,
    w_up,
    w_down,
    out_grad,
):
    rows, width = feats.shape
    peers, slot_count = send_list.shape[1:]
    slots = peers * slot_count
    layers = gate_weight_matrix.shape[0]
    hidden_width = gate_weight_matrix.shape[2]
    parts = lax.axis_size("mp")
    steps = rows // CHUNK

    def swap(blocks):
        return lax.all_to_all(blocks, "dom", split_axis=0, concat_axis=0, tiled=True)

    def exchange(outgoing):
        return swap(outgoing.reshape(peers, slot_count, width)).reshape(slots, width)

    def chunked(x):
        return x, "rows"

    def fixed(x):
        return x, "whole"

    def near(x):
        return x, "near"

    state_shape, sum_shape = shape((rows, width), BF16), shape((rows, width), F32)
    slot_shape = shape((slots, width), BF16)
    dense_scratch = [
        pltpu.VMEM((rows, rows), BF16),
        pltpu.SMEM((rows // BLOCK + 1,), jnp.int32),
        pltpu.SemaphoreType.DMA((rows // BLOCK,)),
    ]
    tiles, cols = (tile_val, "later"), (tile_col, None)
    row_shape, col_shape = shape((1, slots), jnp.int32), shape((slots, LANES), jnp.int32)
    dw_shape = shape((3 * width, hidden_width), BF16)
    half = pltpu.VMEM((rows, hidden_width), BF16)
    kept_shapes = [half, half, half, pltpu.VMEM((rows, width), BF16)]
    local_flops = 2 * rows * rows * width
    slot_flops = 2 * rows * slots * width
    layer_flops = 6 * rows * width * hidden_width * parts
    count = (cell_count, None)

    outgoing, send_col = call(
        send_kernel,
        steps,
        [fixed(slot_shape), fixed(col_shape)],
        [count, (send_count, None), fixed(send_list), chunked(feats)],
        slot_flops,
        "send",
    )
    outgoing, mine = lax.optimization_barrier((outgoing, (gate_weight_matrix, w_up, w_down)))
    arriving = exchange(outgoing)
    turns = [[(d, (d + t) % parts) for d in range(parts)] for t in range(1, parts)]
    held = [mine] + [tuple(lax.ppermute(w, "mp", turn) for w in mine) for turn in turns]

    def weights(layer):
        return [(w, Layer(layer)) for trio in held for w in trio]

    state, total, send_row, recv_row, recv_col = call(
        first_local_kernel,
        steps,
        [
            fixed(state_shape),
            chunked(sum_shape),
            fixed(row_shape),
            fixed(row_shape),
            fixed(col_shape),
        ],
        [
            count,
            (send_count, None),
            cols,
            fixed(send_list),
            fixed(recv_list),
            fixed(feats),
            tiles,
        ],
        local_flops,
        "first_local",
        dense_scratch,
    )
    kept = []
    for layer in range(layers - 1):
        acts, state, outgoing = call(
            functools.partial(forward_kernel, parts),
            steps,
            [chunked(state_shape), chunked(state_shape), fixed(slot_shape)],
            [count, fixed(send_col), fixed(recv_row), near(arriving), *weights(layer), chunked(total), chunked(state)],
            layer_flops + 2 * slot_flops,
            "forward",
        )
        kept.append(acts)
        arriving = exchange(outgoing)
        (total,) = call(
            local_kernel, steps, [chunked(sum_shape)], [cols, fixed(state), tiles], local_flops, "local", dense_scratch
        )
    final, agg, outgoing, dw = call(
        functools.partial(turn_kernel, parts),
        steps,
        [chunked(state_shape), chunked(state_shape), fixed(slot_shape), fixed(dw_shape)],
        [
            count, fixed(recv_col), fixed(recv_row), near(arriving), *weights(layers - 1), chunked(total),
            chunked(state), chunked(out_grad),
        ],
        3 * layer_flops + 2 * slot_flops,
        "turn",
        [pltpu.VMEM((rows, width), BF16), *kept_shapes],
    )
    piece = dw_shape.shape[0] // peers
    both_shape = shape((peers, slot_count + piece, width), BF16)

    def turned_local(agg, upstream):
        return call(
            turned_local_kernel,
            steps,
            [chunked(sum_shape)],
            [count, cols, fixed(agg), chunked(upstream), tiles],
            local_flops,
            "turned_local",
            dense_scratch,
        )[0]

    def added(pieces):
        return jnp.sum(pieces.astype(F32), axis=0).astype(BF16)

    arriving = exchange(outgoing)
    total = turned_local(agg, out_grad)
    reduced = [None] * layers
    for layer in reversed(range(layers - 1)):
        if layer == layers - 2:
            total, arriving, dw = lax.optimization_barrier((total, arriving, dw))
            reduced[layer + 1] = added(swap(dw.reshape(peers, piece, width)))
        upstream, agg, both = call(
            functools.partial(backward_kernel, parts),
            steps,
            [chunked(sum_shape), chunked(state_shape), (both_shape, "later")],
            [
                count, fixed(recv_col), fixed(send_row), near(arriving), *weights(layer), chunked(total),
                chunked(kept[layer]),
            ],
            3 * layer_flops + 2 * slot_flops,
            "backward",
            [
                pltpu.VMEM(slot_shape.shape, BF16),
                pltpu.VMEM(dw_shape.shape, BF16),
                pltpu.SemaphoreType.DMA((peers,)),
                *kept_shapes,
            ],
        )
        both, reduced = lax.optimization_barrier((both, reduced))
        both = swap(both)
        total = turned_local(agg, upstream)
        arriving = both[:, :slot_count].reshape(slots, width)
        reduced[layer] = added(both[:, slot_count:])
    own = jnp.concatenate(reduced)
    full = swap(jnp.broadcast_to(own[None], (peers, *own.shape)))
    (feat_grad,) = call(
        last_kernel,
        steps,
        [chunked(sum_shape)],
        [count, fixed(send_row), near(arriving), chunked(total)],
        slot_flops,
        "last",
    )
    full = full.reshape(peers, layers, piece, width).swapaxes(0, 1).reshape(layers, 3, width, hidden_width)
    full = full.swapaxes(0, 1).astype(F32)
    return (final, feat_grad, full[0], full[1], full[2])


def solution(mesh):
    return jax.shard_map(
        local,
        mesh=mesh,
        in_specs=(
            P(("groups", "dom"), None),
            P(("groups", "dom")),
            P(("groups", "dom"), None),
            P(("groups", "dom"), None, None, None),
            P(("groups", "dom"), None, None),
            P(("groups", "dom"), None),
            P(("groups", "dom"), None, None),
            P(None, None, "mp"),
            P(None, None, "mp"),
            P(None, "mp", None),
            P(("groups", "dom"), None),
        ),
        out_specs=(
            P(("groups", "dom"), None),
            P(("groups", "dom"), None),
            P("groups", None, "mp"),
            P("groups", None, "mp"),
            P("groups", "mp", None),
        ),
        check_vma=False,
    )
```

```python
import functools

import jax
import jax.numpy as jnp
from jax import lax
from jax.experimental import pallas as pl
from jax.experimental.pallas import tpu as pltpu
from jax.sharding import PartitionSpec as P

BF16 = jnp.bfloat16
F32 = jnp.float32
LANES = 128
BLOCK = 128
SMEM = pl.BlockSpec(memory_space=pltpu.SMEM)
SUB = 512
SLOTS = 512
GRANT = 48 * 1024 * 1024
TILE_COPIES = 3


def shape(dims, dtype):
    return jax.ShapeDtypeStruct(tuple(dims), dtype)


class Layer:
    def __init__(self, index):
        self.index = index


class Traffic:
    def __init__(self, ins, outs, in_sems, out_sems):
        self.ins, self.outs, self.in_sems, self.out_sems = ins, outs, in_sems, out_sems
        self.leaving = []
        for k in range(len(ins)):
            if self.moves(k):
                self.arriving(k).start()

    def moves(self, k):
        return self.ins[k][2] not in ("near", "later")

    def arriving(self, k):
        far, near, cut = self.ins[k]
        source = far.at[cut.index] if isinstance(cut, Layer) else far
        return pltpu.make_async_copy(source, near, self.in_sems.at[k])

    def need(self, *names):
        for k, (_, near, _) in enumerate(self.ins):
            if self.moves(k) and any(near is name for name in names):
                self.arriving(k).wait()

    def put(self, k):
        near, far, cut = self.outs[k]
        if cut != "near":
            copy = pltpu.make_async_copy(near, far, self.out_sems.at[k])
            copy.start()
            self.leaving.append(copy)

    def finish(self):
        for copy in self.leaving:
            copy.wait()


def call(kernel, outs, ins, flops, name, scratch=()):
    moved = sum(x.size * x.dtype.itemsize for x, _ in (*ins, *outs))
    far_ins = [(x, cut) for x, cut in ins if cut is not None]
    scalars = len(ins) - len(far_ins)
    staged = [k for k, (_, cut) in enumerate(far_ins) if cut not in ("near", "later")]
    staged_outs = [k for k, (_, cut) in enumerate(outs) if cut not in ("near", "later")]

    def body(*refs):
        fixed, refs = refs[:scalars], refs[scalars:]
        far_in, refs = refs[: len(far_ins)], refs[len(far_ins) :]
        far_out, refs = refs[: len(outs)], refs[len(outs) :]
        near_in, near_out = list(far_in), list(far_out)
        for k in staged:
            near_in[k], *refs = refs
        for k in staged_outs:
            near_out[k], *refs = refs
        in_sems, out_sems, *own = refs
        traffic = Traffic(
            [(f, n, cut) for f, n, (_, cut) in zip(far_in, near_in, far_ins)],
            [(n, f, cut) for n, f, (_, cut) in zip(near_out, far_out, outs)],
            in_sems,
            out_sems,
        )
        shown = [near_out[k] for k in range(len(outs)) if outs[k][1] != "later"]
        kernel(traffic, *fixed, *near_in, *shown, *own)
        traffic.finish()

    def held(x, cut):
        if cut == "scalars":
            return pltpu.SMEM(x.shape, x.dtype)
        return pltpu.VMEM(x.shape[1:] if isinstance(cut, Layer) else x.shape, x.dtype)

    def space(cut):
        return pltpu.VMEM if cut == "near" else pltpu.HBM

    return pl.pallas_call(
        body,
        out_shape=[space(cut)(x.shape, x.dtype) for x, cut in outs],
        in_specs=[SMEM] * scalars + [pl.BlockSpec(memory_space=space(cut)) for _, cut in far_ins],
        out_specs=[pl.BlockSpec(memory_space=space(cut)) for _, cut in outs],
        scratch_shapes=[
            *(held(*far_ins[k]) for k in staged),
            *(held(*outs[k]) for k in staged_outs),
            pltpu.SemaphoreType.DMA((len(far_ins),)),
            pltpu.SemaphoreType.DMA((len(outs),)),
            *scratch,
        ],
        cost_estimate=pl.CostEstimate(flops=flops, bytes_accessed=moved, transcendentals=0),
        compiler_params=pltpu.CompilerParams(vmem_limit_bytes=GRANT),
        name=name,
    )(
        *[x for x, _ in ins[:scalars]],
        *[pltpu.with_memory_space_constraint(x, space(cut)) for x, cut in far_ins],
    )


def pieces_of(rows):
    size = SUB if rows % SUB == 0 else BLOCK
    return [slice(first, first + size) for first in range(0, rows, size)]


def mm(a, b):
    return jnp.dot(a, b, preferred_element_type=F32)


def mm_t(a, b):
    return lax.dot_general(a, b, (((1,), (1,)), ((), ())), preferred_element_type=F32)


def mm_rows(a, b):
    return lax.dot_general(a, b, (((0,), (0,)), ((), ())), preferred_element_type=F32)


def live(count_ref, start, rows, width):
    index = lax.broadcasted_iota(jnp.int32, (rows, width), 0) + start
    return index < count_ref[0]


def fill_columns(col_ref, list_ref, used):
    peers, n = list_ref.shape[1:]
    w = col_ref.shape[0] // peers
    down = lax.broadcasted_iota(jnp.int32, (w, n), 0) + lax.axis_index("mp") * w
    across = lax.broadcasted_iota(jnp.int32, (w, n), 1)

    def step(q, carry):
        line = jnp.broadcast_to(list_ref[0, pl.ds(q, 1), :], (w, n))
        kept = (down == across) & used(q, across, line)
        col = jnp.sum(jnp.where(kept, line + 1, 0), axis=1, keepdims=True) - 1
        col_ref[pl.ds(pl.multiple_of(q * w, w), w), :] = jnp.broadcast_to(col, (w, LANES))
        return carry

    lax.fori_loop(0, peers, step, 0, unroll=4)


def fill_row(parts, row_ref, list_ref, used):
    peers, n = list_ref.shape[1:]
    w = n // parts
    across = lax.broadcasted_iota(jnp.int32, (1, n), 1)
    me = lax.axis_index("mp")
    for q in range(peers):
        line = list_ref[0, q : q + 1, :]
        line = jnp.where(used(q, across, line), line, -1)
        for t in range(parts):
            owner = lax.rem(me + t, parts)
            piece = line[:, :w]
            for p in range(1, parts):
                piece = jnp.where(owner == p, line[:, p * w : (p + 1) * w], piece)
            row_ref[0:1, (t * peers + q) * w : (t * peers + q + 1) * w] = piece


def sent(count_ref, used_ref):
    return lambda q, k, row: (k < used_ref[0, q]) & (row < count_ref[0])


def always(q, k, row):
    return row >= 0


def picks(col, rows):
    lanes = lax.broadcasted_iota(jnp.int32, col.shape, 1)
    return jnp.concatenate(
        [jnp.where(col == lanes + lane, 1.0, 0.0).astype(BF16) for lane in range(0, rows, LANES)], axis=1
    )


def gather_rows(col_ref, source_ref, out_ref):
    slots, rows = out_ref.shape[0], source_ref.shape[0]
    size = min(slots, SLOTS)
    for first in range(0, slots, size):
        at = slice(first, first + size)
        out_ref[at, :] = mm(picks(col_ref[at, :], rows), source_ref[...]).astype(BF16)


def scatter_rows(row_ref, start, rows, arriving):
    slots = row_ref.shape[1] // len(arriving)
    index = lax.broadcasted_iota(jnp.int32, (rows, slots), 0) + start
    total = None
    for t, ref in enumerate(arriving):
        pick = jnp.where(row_ref[0:1, t * slots : (t + 1) * slots] == index, 1.0, 0.0).astype(BF16)
        total = mm(pick, ref[...]) if total is None else total + mm(pick, ref[...])
    return total


def send_kernel(traffic, count_ref, used_ref, list_ref, feats_ref, out_ref, col_ref, pick_ref):
    traffic.need(used_ref, list_ref)
    fill_columns(col_ref, list_ref, sent(count_ref, used_ref))
    traffic.put(1)
    pick_ref[...] = picks(col_ref[...], feats_ref.shape[0])
    traffic.need(feats_ref)
    out_ref[...] = mm(pick_ref[...], feats_ref[...]).astype(BF16)
    traffic.put(0)


class Dense:
    def __init__(self, cols_ref, tile_ref, near_ref, dense_ref, sems):
        self.cols_ref, self.near_ref, self.dense_ref = cols_ref, near_ref, dense_ref
        pieces = sems.shape[0]
        self.size = tile_ref.shape[0] // pieces
        self.copies = [
            pltpu.make_async_copy(
                tile_ref.at[pl.ds(p * self.size, self.size)], near_ref.at[pl.ds(p * self.size, self.size)], sems.at[p]
            )
            for p in range(pieces)
        ]
        for copy in self.copies:
            copy.start()

    def zero(self):
        self.dense_ref[...] = jnp.zeros_like(self.dense_ref)

    def fill(self, p):
        self.copies[p].wait()
        for r in range(p * self.size, (p + 1) * self.size):
            for j in range(self.near_ref.shape[1]):
                at = pl.ds(pl.multiple_of(self.cols_ref[r, j] * BLOCK, BLOCK), BLOCK)
                self.dense_ref[r * BLOCK : (r + 1) * BLOCK, at] = self.near_ref[r, j]


def local_sums(traffic, dense, state_ref, sum_ref, out):
    for p in range(len(dense.copies)):
        dense.fill(p)
    sum_ref[...] = mm(dense.dense_ref[...], state_ref[...]).astype(sum_ref.dtype)
    traffic.put(out)


def first_local_kernel(
    parts, traffic, count_ref, used_ref, cols_ref, send_ref, recv_ref, feats_ref, tile_ref,
    state_ref, sum_ref, send_row_ref, recv_row_ref, recv_col_ref, near_ref, dense_ref, sems,
):
    dense = Dense(cols_ref, tile_ref, near_ref, dense_ref, sems)
    dense.zero()
    rows, width = feats_ref.shape
    traffic.need(send_ref, recv_ref, feats_ref)
    fill_row(parts, send_row_ref, send_ref, sent(count_ref, used_ref))
    fill_row(parts, recv_row_ref, recv_ref, always)
    fill_columns(recv_col_ref, recv_ref, always)
    state_ref[...] = jnp.where(live(count_ref, 0, rows, width), feats_ref[...], jnp.zeros((), BF16))
    for k in (0, 2, 3, 4):
        traffic.put(k)
    local_sums(traffic, dense, state_ref, sum_ref, 1)


def local_kernel(traffic, cols_ref, state_ref, tile_ref, sum_ref, near_ref, dense_ref, sems):
    dense = Dense(cols_ref, tile_ref, near_ref, dense_ref, sems)
    dense.zero()
    local_sums(traffic, dense, state_ref, sum_ref, 0)


def turned_local_kernel(traffic, count_ref, cols_ref, agg_ref, up_ref, tile_ref, sum_ref, near_ref, dense_ref, sems):
    dense = Dense(cols_ref, tile_ref, near_ref, dense_ref, sems)
    dense.zero()
    for p in range(len(dense.copies)):
        dense.fill(p)
    traffic.need(up_ref)
    upstream = jnp.where(live(count_ref, 0, *sum_ref.shape), up_ref[...].astype(F32), 0.0)
    sum_ref[...] = (mm_rows(dense_ref[...], agg_ref[...]) + upstream).astype(sum_ref.dtype)
    traffic.put(0)


def triples(refs, layer):
    return [(refs[i].at[layer], refs[i + 1].at[layer], refs[i + 2]) for i in range(0, len(refs), 3)]


def gates(acts, weights):
    result = []
    for gate_ref, up_ref, _ in weights:
        gate = mm(acts, gate_ref[...])
        up = mm(acts, up_ref[...])
        sig = 0.5 * jnp.tanh(0.5 * gate) + 0.5
        result.append((gate, up, sig, gate * sig))
    return result


def layer_grads(at, acts, terms, down_in, weights, agg_ref, kept):
    agg = None
    for part, ((gate, up, sig, silu), (gate_ref, up_ref, down_ref)) in enumerate(zip(terms, weights)):
        hidden_grad = mm_t(down_in, down_ref[...])
        slope = sig * (1.0 + gate * (1.0 - sig))
        gate_grad = (hidden_grad * up * slope).astype(BF16)
        up_grad = (hidden_grad * silu).astype(BF16)
        more = mm_t(gate_grad, gate_ref[...]) + mm_t(up_grad, up_ref[...])
        agg = more if agg is None else agg + more
        if part == 0:
            for ref, value in zip(kept, ((silu * up).astype(BF16), gate_grad, up_grad, down_in)):
                ref[at, :] = value
    agg_ref[at, :] = agg.astype(BF16)


def weight_grads(acts_ref, kept, dw_ref):
    hidden_ref, gate_ref, up_ref, down_ref = kept
    pairs = ((acts_ref, gate_ref), (acts_ref, up_ref), (hidden_ref, down_ref))
    for k, (left_ref, right_ref) in enumerate(pairs):
        size = left_ref.shape[1]
        dw_ref[k * size : (k + 1) * size, :] = mm_rows(left_ref[...], right_ref[...]).astype(BF16)


def mix(terms, weights):
    mixed = None
    for (gate, up, sig, silu), (_, _, down_ref) in zip(terms, weights):
        part = mm((silu * up).astype(BF16), down_ref[...])
        mixed = part if mixed is None else mixed + part
    return mixed


def forward_kernel(parts, layer, traffic, count_ref, col_ref, row_ref, *refs):
    arriving, refs = refs[:parts], refs[parts:]
    weights = triples(refs[: 3 * parts], layer)
    sum_ref, state_ref, acts_ref, next_ref, out_ref = refs[3 * parts :]
    width = state_ref.shape[1]
    for at in pieces_of(state_ref.shape[0]):
        size = at.stop - at.start
        acts = (sum_ref[at, :].astype(F32) + scatter_rows(row_ref, at.start, size, arriving)).astype(BF16)
        acts_ref[at, :] = acts
        terms = gates(acts, weights)
        if at.start == 0:
            traffic.need(*(down_ref for _, _, down_ref in weights))
        after = state_ref[at, :].astype(F32) + mix(terms, weights)
        next_ref[at, :] = jnp.where(live(count_ref, at.start, size, width), after, 0.0).astype(BF16)
    traffic.put(0)
    gather_rows(col_ref, next_ref, out_ref)
    traffic.put(2)


def turn_kernel(parts, layer, traffic, count_ref, col_ref, row_ref, *refs):
    arriving, refs = refs[:parts], refs[parts:]
    weights = triples(refs[: 3 * parts], layer)
    sum_ref, state_ref, grad_ref, final_ref, agg_ref, out_ref, dw_ref, acts_ref, *kept = refs[3 * parts :]
    width = state_ref.shape[1]
    for at in pieces_of(state_ref.shape[0]):
        size = at.stop - at.start
        acts = (sum_ref[at, :].astype(F32) + scatter_rows(row_ref, at.start, size, arriving)).astype(BF16)
        acts_ref[at, :] = acts
        terms = gates(acts, weights)
        if at.start == 0:
            traffic.need(*(down_ref for _, _, down_ref in weights), grad_ref)
        after = state_ref[at, :].astype(F32) + mix(terms, weights)
        alive = live(count_ref, at.start, size, width)
        final_ref[at, :] = jnp.where(alive, after, 0.0).astype(BF16)
        down_in = jnp.where(alive, grad_ref[at, :], jnp.zeros((), BF16))
        layer_grads(at, acts, terms, down_in, weights, agg_ref, kept)
    traffic.put(0)
    gather_rows(col_ref, agg_ref, out_ref)
    traffic.put(2)
    weight_grads(acts_ref, kept, dw_ref)
    traffic.put(3)


def put_pieces(traffic, k, sources, sem):
    far = traffic.outs[k][1]
    for q in range(far.shape[0]):
        first = 0
        for source in sources:
            rows = source.shape[0] // far.shape[0]
            copy = pltpu.make_async_copy(
                source.at[pl.ds(q * rows, rows)], far.at[q, pl.ds(first, rows)], sem.at[q]
            )
            copy.start()
            traffic.leaving.append(copy)
            first += rows


def backward_kernel(parts, layer, traffic, count_ref, col_ref, row_ref, *refs):
    arriving, refs = refs[:parts], refs[parts:]
    weights = triples(refs[: 3 * parts], layer)
    sum_ref, acts_ref, upstream_ref, agg_ref, out_ref, dw_ref, sem, *kept = refs[3 * parts :]
    rows, width = acts_ref.shape
    for at in pieces_of(rows):
        size = at.stop - at.start
        carried = sum_ref[at, :].astype(F32) + scatter_rows(row_ref, at.start, size, arriving)
        upstream_ref[at, :] = jnp.where(live(count_ref, at.start, size, width), carried, 0.0).astype(BF16)
    traffic.put(0)
    traffic.need(acts_ref, *(down_ref for _, _, down_ref in weights))
    for at in pieces_of(rows):
        acts = acts_ref[at, :]
        layer_grads(at, acts, gates(acts, weights), upstream_ref[at, :], weights, agg_ref, kept)
    gather_rows(col_ref, agg_ref, out_ref)
    weight_grads(acts_ref, (*kept, upstream_ref), dw_ref)
    put_pieces(traffic, 2, (out_ref, dw_ref), sem)


def last_kernel(traffic, count_ref, row_ref, *refs):
    *arriving, sum_ref, out_ref = refs
    width = out_ref.shape[1]
    for at in pieces_of(out_ref.shape[0]):
        size = at.stop - at.start
        carried = sum_ref[at, :].astype(F32) + scatter_rows(row_ref, at.start, size, arriving)
        out_ref[at, :] = jnp.where(live(count_ref, at.start, size, width), carried, 0.0)
    traffic.put(0)


def local(
    feats,
    cell_count,
    tile_col,
    tile_val,
    send_list,
    send_count,
    recv_list,
    gate_weight_matrix,
    w_up,
    w_down,
    out_grad,
):
    rows, width = feats.shape
    peers, slot_count = send_list.shape[1:]
    slots = peers * slot_count
    layers = gate_weight_matrix.shape[0]
    hidden_width = gate_weight_matrix.shape[2]
    parts = lax.axis_size("mp")

    turns = [[(d, (d - t) % parts) for d in range(parts)] for t in range(1, parts)]

    def swap(blocks):
        return lax.all_to_all(blocks, "dom", split_axis=0, concat_axis=0, tiled=True)

    def share(rows):
        rows = rows.reshape(slots // parts, width)
        return [rows] + [lax.ppermute(rows, "mp", turn) for turn in turns]

    def exchange(outgoing):
        return swap(outgoing.reshape(peers, slot_count // parts, width))

    def share_after(total, moved):
        total, moved = lax.optimization_barrier((total, moved))
        return total, share(moved)

    def far(x):
        return x, "far"

    def near(x):
        return x, "near"

    state_shape, sum_shape = shape((rows, width), BF16), shape((rows, width), BF16)
    slot_shape = shape((slots // parts, width), BF16)
    dense_scratch = [
        pltpu.VMEM(tile_val.shape, BF16),
        pltpu.VMEM((rows, rows), BF16),
        pltpu.SemaphoreType.DMA((TILE_COPIES,)),
    ]
    tiles, cols = (tile_val, "later"), (tile_col, None)
    row_shape, col_shape = shape((1, slots), jnp.int32), shape((slots // parts, LANES), jnp.int32)
    dw_shape = shape((3 * width, hidden_width), BF16)
    half = pltpu.VMEM((rows, hidden_width), BF16)
    kept_shapes = [half, half, half, pltpu.VMEM((rows, width), BF16)]
    local_flops = 2 * rows * rows * width
    slot_flops = 2 * rows * slots * width
    layer_flops = 6 * rows * width * hidden_width * parts
    count = (cell_count, None)

    outgoing, send_col = call(
        send_kernel,
        [far(slot_shape), near(col_shape)],
        [count, (send_count, "scalars"), far(send_list), far(feats)],
        slot_flops,
        "send",
        [pltpu.VMEM((slots // parts, rows), BF16)],
    )
    outgoing, mine = lax.optimization_barrier((outgoing, (gate_weight_matrix, w_up, w_down)))
    arriving = exchange(outgoing)
    held = [mine] + [tuple(lax.ppermute(w, "mp", turn) for w in mine) for turn in turns]

    def weights(layer):
        return [spec for gate, up, down in held for spec in (near(gate), near(up), (down, Layer(layer)))]

    state, total, send_row, recv_row, recv_col = call(
        functools.partial(first_local_kernel, parts),
        [
            near(state_shape),
            near(sum_shape),
            near(row_shape),
            near(row_shape),
            near(col_shape),
        ],
        [
            count,
            (send_count, None),
            cols,
            far(send_list),
            far(recv_list),
            far(feats),
            tiles,
        ],
        local_flops,
        "first_local",
        dense_scratch,
    )
    total, arriving = share_after(total, arriving)
    kept = []
    for layer in range(layers - 1):
        acts, state, outgoing = call(
            functools.partial(forward_kernel, parts, layer),
            [far(state_shape), near(state_shape), far(slot_shape)],
            [count, near(send_col), near(recv_row), *map(near, arriving), *weights(layer), near(total), near(state)],
            layer_flops + 2 * slot_flops,
            "forward",
        )
        kept.append(acts)
        arriving = exchange(outgoing)
        (total,) = call(
            local_kernel, [near(sum_shape)], [cols, near(state), tiles], local_flops, "local", dense_scratch
        )
        total, arriving = share_after(total, arriving)
    final, agg, outgoing, dw = call(
        functools.partial(turn_kernel, parts, layers - 1),
        [far(state_shape), near(state_shape), far(slot_shape), far(dw_shape)],
        [
            count, near(recv_col), near(recv_row), *map(near, arriving), *weights(layers - 1), near(total),
            near(state), far(out_grad),
        ],
        3 * layer_flops + 2 * slot_flops,
        "turn",
        [pltpu.VMEM((rows, width), BF16), *kept_shapes],
    )
    piece = dw_shape.shape[0] // peers
    own_slots = slot_count // parts
    both_shape = shape((peers, own_slots + piece, width), BF16)

    def turned_local(agg, upstream):
        return call(
            turned_local_kernel,
            [near(sum_shape)],
            [count, cols, near(agg), far(upstream), tiles],
            local_flops,
            "turned_local",
            dense_scratch,
        )[0]

    def added(pieces):
        return jnp.sum(pieces.astype(F32), axis=0).astype(BF16)

    arriving = exchange(outgoing)
    total, arriving = share_after(turned_local(agg, out_grad), arriving)
    reduced = [None] * layers
    for layer in reversed(range(layers - 1)):
        if layer == layers - 2:
            arriving, dw = lax.optimization_barrier((arriving, dw))
            pieces = swap(dw.reshape(peers, piece, width))
        upstream, agg, both = call(
            functools.partial(backward_kernel, parts, layer),
            [far(sum_shape), near(state_shape), (both_shape, "later")],
            [
                count, near(recv_col), near(send_row), *map(near, arriving), *weights(layer), near(total),
                far(kept[layer]),
            ],
            3 * layer_flops + 2 * slot_flops,
            "backward",
            [
                pltpu.VMEM(slot_shape.shape, BF16),
                pltpu.VMEM(dw_shape.shape, BF16),
                pltpu.SemaphoreType.DMA((peers,)),
                *kept_shapes[:3],
            ],
        )
        if layer == layers - 2:
            both, pieces = lax.optimization_barrier((both, pieces))
            reduced[layer + 1] = added(pieces)
        both = swap(both)
        total, both = lax.optimization_barrier((turned_local(agg, upstream), both))
        arriving = share(both[:, :own_slots])
        reduced[layer] = added(both[:, own_slots:])
    own = jnp.concatenate(reduced)
    full = swap(jnp.broadcast_to(own[None], (peers, *own.shape)))
    (feat_grad,) = call(
        last_kernel,
        [far(shape((rows, width), F32))],
        [count, near(send_row), *map(near, arriving), near(total)],
        slot_flops,
        "last",
    )
    full = full.reshape(peers, layers, piece, width).swapaxes(0, 1).reshape(layers, 3, width, hidden_width)
    full = full.swapaxes(0, 1).astype(F32)
    return (final, feat_grad, full[0], full[1], full[2])


def solution(mesh):
    return jax.shard_map(
        local,
        mesh=mesh,
        in_specs=(
            P(("groups", "dom"), None),
            P(("groups", "dom")),
            P(("groups", "dom"), None),
            P(("groups", "dom"), None, None, None),
            P(("groups", "dom"), None, None),
            P(("groups", "dom"), None),
            P(("groups", "dom"), None, None),
            P(None, None, "mp"),
            P(None, None, "mp"),
            P(None, "mp", None),
            P(("groups", "dom"), None),
        ),
        out_specs=(
            P(("groups", "dom"), None),
            P(("groups", "dom"), None),
            P("groups", None, "mp"),
            P("groups", None, "mp"),
            P("groups", "mp", None),
        ),
        check_vma=False,
    )
```

```python
import functools

import jax
import jax.numpy as jnp
from jax import lax
from jax.experimental import pallas as pl
from jax.experimental.pallas import tpu as pltpu
from jax.sharding import PartitionSpec as P

BF16 = jnp.bfloat16
F32 = jnp.float32
LANES = 128
BLOCK = 128
SMEM = pl.BlockSpec(memory_space=pltpu.SMEM)
SUB = 512
SLOTS = 512
GRANT = 48 * 1024 * 1024
TILE_COPIES = 3


def shape(dims, dtype):
    return jax.ShapeDtypeStruct(tuple(dims), dtype)


class Layer:
    def __init__(self, index):
        self.index = index


class Traffic:
    def __init__(self, ins, outs, in_sems, out_sems):
        self.ins, self.outs, self.in_sems, self.out_sems = ins, outs, in_sems, out_sems
        self.leaving = []
        for k in range(len(ins)):
            if self.moves(k):
                self.arriving(k).start()

    def moves(self, k):
        return self.ins[k][2] not in ("near", "later")

    def arriving(self, k):
        far, near, cut = self.ins[k]
        source = far.at[cut.index] if isinstance(cut, Layer) else far
        return pltpu.make_async_copy(source, near, self.in_sems.at[k])

    def need(self, *names):
        for k, (_, near, _) in enumerate(self.ins):
            if self.moves(k) and any(near is name for name in names):
                self.arriving(k).wait()

    def put(self, k):
        near, far, cut = self.outs[k]
        if cut != "near":
            copy = pltpu.make_async_copy(near, far, self.out_sems.at[k])
            copy.start()
            self.leaving.append(copy)

    def finish(self):
        for copy in self.leaving:
            copy.wait()


def call(kernel, outs, ins, flops, name, scratch=()):
    moved = sum(x.size * x.dtype.itemsize for x, _ in (*ins, *outs))
    far_ins = [(x, cut) for x, cut in ins if cut is not None]
    scalars = len(ins) - len(far_ins)
    staged = [k for k, (_, cut) in enumerate(far_ins) if cut not in ("near", "later")]
    staged_outs = [k for k, (_, cut) in enumerate(outs) if cut not in ("near", "later")]

    def body(*refs):
        fixed, refs = refs[:scalars], refs[scalars:]
        far_in, refs = refs[: len(far_ins)], refs[len(far_ins) :]
        far_out, refs = refs[: len(outs)], refs[len(outs) :]
        near_in, near_out = list(far_in), list(far_out)
        for k in staged:
            near_in[k], *refs = refs
        for k in staged_outs:
            near_out[k], *refs = refs
        in_sems, out_sems, *own = refs
        traffic = Traffic(
            [(f, n, cut) for f, n, (_, cut) in zip(far_in, near_in, far_ins)],
            [(n, f, cut) for n, f, (_, cut) in zip(near_out, far_out, outs)],
            in_sems,
            out_sems,
        )
        shown = [near_out[k] for k in range(len(outs)) if outs[k][1] != "later"]
        kernel(traffic, *fixed, *near_in, *shown, *own)
        traffic.finish()

    def held(x, cut):
        if cut == "scalars":
            return pltpu.SMEM(x.shape, x.dtype)
        return pltpu.VMEM(x.shape[1:] if isinstance(cut, Layer) else x.shape, x.dtype)

    def space(cut):
        return pltpu.VMEM if cut == "near" else pltpu.HBM

    return pl.pallas_call(
        body,
        out_shape=[space(cut)(x.shape, x.dtype) for x, cut in outs],
        in_specs=[SMEM] * scalars + [pl.BlockSpec(memory_space=space(cut)) for _, cut in far_ins],
        out_specs=[pl.BlockSpec(memory_space=space(cut)) for _, cut in outs],
        scratch_shapes=[
            *(held(*far_ins[k]) for k in staged),
            *(held(*outs[k]) for k in staged_outs),
            pltpu.SemaphoreType.DMA((len(far_ins),)),
            pltpu.SemaphoreType.DMA((len(outs),)),
            *scratch,
        ],
        cost_estimate=pl.CostEstimate(flops=flops, bytes_accessed=moved, transcendentals=0),
        compiler_params=pltpu.CompilerParams(vmem_limit_bytes=GRANT),
        name=name,
    )(
        *[x for x, _ in ins[:scalars]],
        *[pltpu.with_memory_space_constraint(x, space(cut)) for x, cut in far_ins],
    )


def pieces_of(rows):
    size = SUB if rows % SUB == 0 else BLOCK
    return [slice(first, first + size) for first in range(0, rows, size)]


def mm(a, b):
    return jnp.dot(a, b, preferred_element_type=F32)


def mm_t(a, b):
    return lax.dot_general(a, b, (((1,), (1,)), ((), ())), preferred_element_type=F32)


def mm_rows(a, b):
    return lax.dot_general(a, b, (((0,), (0,)), ((), ())), preferred_element_type=F32)


def live(count_ref, start, rows, width):
    index = lax.broadcasted_iota(jnp.int32, (rows, width), 0) + start
    return index < count_ref[0]


def fill_columns(col_ref, list_ref, used):
    peers, n = list_ref.shape[1:]
    w = col_ref.shape[0] // peers
    down = lax.broadcasted_iota(jnp.int32, (w, n), 0) + lax.axis_index("mp") * w
    across = lax.broadcasted_iota(jnp.int32, (w, n), 1)

    def step(q, carry):
        line = jnp.broadcast_to(list_ref[0, pl.ds(q, 1), :], (w, n))
        kept = (down == across) & used(q, across, line)
        col = jnp.sum(jnp.where(kept, line + 1, 0), axis=1, keepdims=True) - 1
        col_ref[pl.ds(pl.multiple_of(q * w, w), w), :] = jnp.broadcast_to(col, (w, LANES))
        return carry

    lax.fori_loop(0, peers, step, 0, unroll=4)


def fill_row(parts, row_ref, list_ref, used):
    peers, n = list_ref.shape[1:]
    w = n // parts
    across = lax.broadcasted_iota(jnp.int32, (1, n), 1)
    me = lax.axis_index("mp")
    for q in range(peers):
        line = list_ref[0, q : q + 1, :]
        line = jnp.where(used(q, across, line), line, -1)
        for t in range(parts):
            owner = lax.rem(me + t, parts)
            piece = line[:, :w]
            for p in range(1, parts):
                piece = jnp.where(owner == p, line[:, p * w : (p + 1) * w], piece)
            row_ref[0:1, (t * peers + q) * w : (t * peers + q + 1) * w] = piece


def sent(count_ref, used_ref):
    return lambda q, k, row: (k < used_ref[0, q]) & (row < count_ref[0])


def always(q, k, row):
    return row >= 0


def picks(col, rows):
    lanes = lax.broadcasted_iota(jnp.int32, col.shape, 1)
    return jnp.concatenate(
        [jnp.where(col == lanes + lane, 1.0, 0.0).astype(BF16) for lane in range(0, rows, LANES)], axis=1
    )


def gather_rows(col_ref, source_ref, out_ref):
    slots, rows = out_ref.shape[0], source_ref.shape[0]
    size = min(slots, SLOTS)
    for first in range(0, slots, size):
        at = slice(first, first + size)
        out_ref[at, :] = mm(picks(col_ref[at, :], rows), source_ref[...]).astype(BF16)


def scatter_rows(row_ref, start, rows, arriving):
    slots = row_ref.shape[1] // len(arriving)
    index = lax.broadcasted_iota(jnp.int32, (rows, slots), 0) + start
    total = None
    for t, ref in enumerate(arriving):
        pick = jnp.where(row_ref[0:1, t * slots : (t + 1) * slots] == index, 1.0, 0.0).astype(BF16)
        total = mm(pick, ref[...]) if total is None else total + mm(pick, ref[...])
    return total


def send_kernel(traffic, count_ref, used_ref, list_ref, feats_ref, out_ref, col_ref, pick_ref):
    traffic.need(used_ref, list_ref)
    fill_columns(col_ref, list_ref, sent(count_ref, used_ref))
    traffic.put(1)
    pick_ref[...] = picks(col_ref[...], feats_ref.shape[0])
    traffic.need(feats_ref)
    out_ref[...] = mm(pick_ref[...], feats_ref[...]).astype(BF16)
    traffic.put(0)


class Dense:
    def __init__(self, cols_ref, tile_ref, near_ref, dense_ref, sems):
        self.cols_ref, self.near_ref, self.dense_ref = cols_ref, near_ref, dense_ref
        pieces = sems.shape[0]
        self.size = tile_ref.shape[0] // pieces
        self.copies = [
            pltpu.make_async_copy(
                tile_ref.at[pl.ds(p * self.size, self.size)], near_ref.at[pl.ds(p * self.size, self.size)], sems.at[p]
            )
            for p in range(pieces)
        ]
        for copy in self.copies:
            copy.start()

    def zero(self):
        self.dense_ref[...] = jnp.zeros_like(self.dense_ref)

    def fill(self, p):
        self.copies[p].wait()
        for r in range(p * self.size, (p + 1) * self.size):
            for j in range(self.near_ref.shape[1]):
                at = pl.ds(pl.multiple_of(self.cols_ref[r, j] * BLOCK, BLOCK), BLOCK)
                self.dense_ref[r * BLOCK : (r + 1) * BLOCK, at] = self.near_ref[r, j]


def local_sums(traffic, dense, state_ref, sum_ref, out):
    for p in range(len(dense.copies)):
        dense.fill(p)
    sum_ref[...] = mm(dense.dense_ref[...], state_ref[...]).astype(sum_ref.dtype)
    traffic.put(out)


def first_local_kernel(
    parts, traffic, count_ref, used_ref, cols_ref, send_ref, recv_ref, feats_ref, tile_ref,
    sum_ref, send_row_ref, recv_row_ref, recv_col_ref, near_ref, dense_ref, sems, state_ref,
):
    dense = Dense(cols_ref, tile_ref, near_ref, dense_ref, sems)
    dense.zero()
    rows, width = feats_ref.shape
    traffic.need(send_ref, recv_ref, feats_ref)
    fill_row(parts, send_row_ref, send_ref, sent(count_ref, used_ref))
    fill_row(parts, recv_row_ref, recv_ref, always)
    fill_columns(recv_col_ref, recv_ref, always)
    state_ref[...] = jnp.where(live(count_ref, 0, rows, width), feats_ref[...], jnp.zeros((), BF16))
    for k in (1, 2, 3):
        traffic.put(k)
    local_sums(traffic, dense, state_ref, sum_ref, 0)


def local_kernel(traffic, cols_ref, state_ref, tile_ref, sum_ref, near_ref, dense_ref, sems):
    dense = Dense(cols_ref, tile_ref, near_ref, dense_ref, sems)
    dense.zero()
    local_sums(traffic, dense, state_ref, sum_ref, 0)


def turned_local_kernel(traffic, count_ref, cols_ref, agg_ref, up_ref, tile_ref, sum_ref, near_ref, dense_ref, sems):
    dense = Dense(cols_ref, tile_ref, near_ref, dense_ref, sems)
    dense.zero()
    for p in range(len(dense.copies)):
        dense.fill(p)
    traffic.need(up_ref)
    upstream = jnp.where(live(count_ref, 0, *sum_ref.shape), up_ref[...].astype(F32), 0.0)
    sum_ref[...] = (mm_rows(dense_ref[...], agg_ref[...]) + upstream).astype(sum_ref.dtype)
    traffic.put(0)


def triples(refs, layer):
    return [(refs[i].at[layer], refs[i + 1].at[layer], refs[i + 2]) for i in range(0, len(refs), 3)]


def gates(acts, weights):
    result = []
    for gate_ref, up_ref, _ in weights:
        gate = mm(acts, gate_ref[...])
        up = mm(acts, up_ref[...])
        sig = 0.5 * jnp.tanh(0.5 * gate) + 0.5
        result.append((gate, up, sig, gate * sig))
    return result


def layer_grads(at, acts, terms, down_in, weights, agg_ref, kept):
    agg = None
    for part, ((gate, up, sig, silu), (gate_ref, up_ref, down_ref)) in enumerate(zip(terms, weights)):
        hidden_grad = mm_t(down_in, down_ref[...])
        slope = sig + silu * (1.0 - sig)
        gate_grad = (hidden_grad * up * slope).astype(BF16)
        up_grad = (hidden_grad * silu).astype(BF16)
        more = mm_t(gate_grad, gate_ref[...]) + mm_t(up_grad, up_ref[...])
        agg = more if agg is None else agg + more
        if part == 0:
            hidden_ref, both_ref, *down = kept
            half = gate_grad.shape[1]
            hidden_ref[at, :] = (silu * up).astype(BF16)
            both_ref[at, :half] = gate_grad
            both_ref[at, half:] = up_grad
            for ref in down:
                ref[at, :] = down_in
    agg_ref[at, :] = agg.astype(BF16)


def weight_grads(acts_ref, kept, dw_ref):
    hidden_ref, both_ref, down_ref = kept
    size = acts_ref.shape[1]
    half = both_ref.shape[1] // 2
    both = mm_rows(acts_ref[...], both_ref[...]).astype(BF16)
    dw_ref[:size, :] = both[:, :half]
    dw_ref[size : 2 * size, :] = both[:, half:]
    dw_ref[2 * size :, :] = mm_rows(hidden_ref[...], down_ref[...]).astype(BF16)


def mix(terms, weights):
    mixed = None
    for (gate, up, sig, silu), (_, _, down_ref) in zip(terms, weights):
        part = mm((silu * up).astype(BF16), down_ref[...])
        mixed = part if mixed is None else mixed + part
    return mixed


def forward_kernel(parts, layer, traffic, count_ref, col_ref, row_ref, *refs):
    arriving, refs = refs[:parts], refs[parts:]
    weights = triples(refs[: 3 * parts], layer)
    sum_ref, state_ref, acts_ref, next_ref, out_ref = refs[3 * parts :]
    width = state_ref.shape[1]
    for at in pieces_of(state_ref.shape[0]):
        size = at.stop - at.start
        acts = (sum_ref[at, :].astype(F32) + scatter_rows(row_ref, at.start, size, arriving)).astype(BF16)
        acts_ref[at, :] = acts
        terms = gates(acts, weights)
        if at.start == 0:
            traffic.need(*(down_ref for _, _, down_ref in weights), state_ref)
        after = state_ref[at, :].astype(F32) + mix(terms, weights)
        next_ref[at, :] = jnp.where(live(count_ref, at.start, size, width), after, 0.0).astype(BF16)
    traffic.put(0)
    traffic.need(col_ref)
    gather_rows(col_ref, next_ref, out_ref)
    traffic.put(2)


def turn_kernel(parts, layer, traffic, count_ref, col_ref, row_ref, *refs):
    arriving, refs = refs[:parts], refs[parts:]
    weights = triples(refs[: 3 * parts], layer)
    sum_ref, state_ref, grad_ref, final_ref, agg_ref, out_ref, dw_ref, acts_ref, *kept = refs[3 * parts :]
    width = state_ref.shape[1]
    for at in pieces_of(state_ref.shape[0]):
        size = at.stop - at.start
        acts = (sum_ref[at, :].astype(F32) + scatter_rows(row_ref, at.start, size, arriving)).astype(BF16)
        acts_ref[at, :] = acts
        terms = gates(acts, weights)
        if at.start == 0:
            traffic.need(*(down_ref for _, _, down_ref in weights), state_ref, grad_ref)
        after = state_ref[at, :].astype(F32) + mix(terms, weights)
        alive = live(count_ref, at.start, size, width)
        final_ref[at, :] = jnp.where(alive, after, 0.0).astype(BF16)
        down_in = jnp.where(alive, grad_ref[at, :], jnp.zeros((), BF16))
        layer_grads(at, acts, terms, down_in, weights, agg_ref, kept)
    traffic.put(0)
    traffic.need(col_ref)
    gather_rows(col_ref, agg_ref, out_ref)
    traffic.put(2)
    weight_grads(acts_ref, kept, dw_ref)
    traffic.put(3)


def put_pieces(traffic, k, sources, sem):
    far = traffic.outs[k][1]
    for q in range(far.shape[0]):
        first = 0
        for source in sources:
            rows = source.shape[0] // far.shape[0]
            copy = pltpu.make_async_copy(
                source.at[pl.ds(q * rows, rows)], far.at[q, pl.ds(first, rows)], sem.at[q]
            )
            copy.start()
            traffic.leaving.append(copy)
            first += rows


def backward_kernel(parts, layer, traffic, count_ref, col_ref, row_ref, *refs):
    arriving, refs = refs[:parts], refs[parts:]
    weights = triples(refs[: 3 * parts], layer)
    sum_ref, acts_ref, upstream_ref, agg_ref, out_ref, dw_ref, sem, *kept = refs[3 * parts :]
    rows, width = acts_ref.shape
    for at in pieces_of(rows):
        size = at.stop - at.start
        carried = sum_ref[at, :].astype(F32) + scatter_rows(row_ref, at.start, size, arriving)
        upstream_ref[at, :] = jnp.where(live(count_ref, at.start, size, width), carried, 0.0).astype(BF16)
    traffic.put(0)
    traffic.need(acts_ref, *(down_ref for _, _, down_ref in weights))
    for at in pieces_of(rows):
        acts = acts_ref[at, :]
        layer_grads(at, acts, gates(acts, weights), upstream_ref[at, :], weights, agg_ref, kept)
    traffic.need(col_ref)
    gather_rows(col_ref, agg_ref, out_ref)
    weight_grads(acts_ref, (*kept, upstream_ref), dw_ref)
    put_pieces(traffic, 2, (out_ref, dw_ref), sem)


def last_kernel(traffic, count_ref, row_ref, *refs):
    *arriving, sum_ref, out_ref = refs
    width = out_ref.shape[1]
    for at in pieces_of(out_ref.shape[0]):
        size = at.stop - at.start
        carried = sum_ref[at, :].astype(F32) + scatter_rows(row_ref, at.start, size, arriving)
        out_ref[at, :] = jnp.where(live(count_ref, at.start, size, width), carried, 0.0)
    traffic.put(0)


def local(
    feats,
    cell_count,
    tile_col,
    tile_val,
    send_list,
    send_count,
    recv_list,
    gate_weight_matrix,
    w_up,
    w_down,
    out_grad,
):
    rows, width = feats.shape
    peers, slot_count = send_list.shape[1:]
    slots = peers * slot_count
    layers = gate_weight_matrix.shape[0]
    hidden_width = gate_weight_matrix.shape[2]
    parts = lax.axis_size("mp")

    turns = [[(d, (d - t) % parts) for d in range(parts)] for t in range(1, parts)]

    def swap(blocks):
        return lax.all_to_all(blocks, "dom", split_axis=0, concat_axis=0, tiled=True)

    def share(rows):
        rows = rows.reshape(slots // parts, width)
        return [rows] + [lax.ppermute(rows, "mp", turn) for turn in turns]

    def exchange(outgoing):
        return swap(outgoing.reshape(peers, slot_count // parts, width))

    def share_after(total, moved):
        total, moved = lax.optimization_barrier((total, moved))
        return total, share(moved)

    def far(x):
        return x, "far"

    def near(x):
        return x, "near"

    state_shape, sum_shape = shape((rows, width), BF16), shape((rows, width), BF16)
    slot_shape = shape((slots // parts, width), BF16)
    dense_scratch = [
        pltpu.VMEM(tile_val.shape, BF16),
        pltpu.VMEM((rows, rows), BF16),
        pltpu.SemaphoreType.DMA((TILE_COPIES,)),
    ]
    tiles, cols = (tile_val, "later"), (tile_col, None)
    row_shape, col_shape = shape((1, slots), jnp.int32), shape((slots // parts, LANES), jnp.int32)
    dw_shape = shape((3 * width, hidden_width), BF16)
    half = pltpu.VMEM((rows, hidden_width), BF16)
    kept_shapes = [half, pltpu.VMEM((rows, 2 * hidden_width), BF16), pltpu.VMEM((rows, width), BF16)]
    local_flops = 2 * rows * rows * width
    slot_flops = 2 * rows * slots * width
    layer_flops = 6 * rows * width * hidden_width * parts
    count = (cell_count, None)

    outgoing, send_col = call(
        send_kernel,
        [far(slot_shape), far(col_shape)],
        [count, (send_count, "scalars"), far(send_list), far(feats)],
        slot_flops,
        "send",
        [pltpu.VMEM((slots // parts, rows), BF16)],
    )
    outgoing, mine = lax.optimization_barrier((outgoing, (gate_weight_matrix, w_up, w_down)))
    arriving = exchange(outgoing)
    held = [mine] + [tuple(lax.ppermute(w, "mp", turn) for w in mine) for turn in turns]

    def weights(layer):
        return [spec for gate, up, down in held for spec in (near(gate), near(up), (down, Layer(layer)))]

    total, send_row, recv_row, recv_col = call(
        functools.partial(first_local_kernel, parts),
        [
            near(sum_shape),
            near(row_shape),
            near(row_shape),
            far(col_shape),
        ],
        [
            count,
            (send_count, None),
            cols,
            far(send_list),
            far(recv_list),
            far(feats),
            tiles,
        ],
        local_flops,
        "first_local",
        [*dense_scratch, pltpu.VMEM((rows, width), BF16)],
    )
    total, arriving = share_after(total, arriving)
    state = far(feats)
    kept = []
    for layer in range(layers - 1):
        acts, after, outgoing = call(
            functools.partial(forward_kernel, parts, layer),
            [far(state_shape), near(state_shape), far(slot_shape)],
            [count, far(send_col), near(recv_row), *map(near, arriving), *weights(layer), near(total), state],
            layer_flops + 2 * slot_flops,
            "forward",
        )
        kept.append(acts)
        state = near(after)
        arriving = exchange(outgoing)
        (total,) = call(
            local_kernel, [near(sum_shape)], [cols, state, tiles], local_flops, "local", dense_scratch
        )
        total, arriving = share_after(total, arriving)
    final, agg, outgoing, dw = call(
        functools.partial(turn_kernel, parts, layers - 1),
        [far(state_shape), near(state_shape), far(slot_shape), far(dw_shape)],
        [
            count, far(recv_col), near(recv_row), *map(near, arriving), *weights(layers - 1), near(total),
            state, far(out_grad),
        ],
        3 * layer_flops + 2 * slot_flops,
        "turn",
        [pltpu.VMEM((rows, width), BF16), *kept_shapes],
    )
    piece = dw_shape.shape[0] // peers
    own_slots = slot_count // parts
    both_shape = shape((peers, own_slots + piece, width), BF16)

    def turned_local(agg, upstream):
        return call(
            turned_local_kernel,
            [near(sum_shape)],
            [count, cols, near(agg), far(upstream), tiles],
            local_flops,
            "turned_local",
            dense_scratch,
        )[0]

    def added(pieces):
        return jnp.sum(pieces.astype(F32), axis=0).astype(BF16)

    arriving = exchange(outgoing)
    total, arriving = share_after(turned_local(agg, out_grad), arriving)
    reduced = [None] * layers
    for layer in reversed(range(layers - 1)):
        if layer == layers - 2:
            arriving, dw = lax.optimization_barrier((arriving, dw))
            pieces = swap(dw.reshape(peers, piece, width))
        upstream, agg, both = call(
            functools.partial(backward_kernel, parts, layer),
            [far(sum_shape), near(state_shape), (both_shape, "later")],
            [
                count, far(recv_col), near(send_row), *map(near, arriving), *weights(layer), near(total),
                far(kept[layer]),
            ],
            3 * layer_flops + 2 * slot_flops,
            "backward",
            [
                pltpu.VMEM(slot_shape.shape, BF16),
                pltpu.VMEM(dw_shape.shape, BF16),
                pltpu.SemaphoreType.DMA((peers,)),
                *kept_shapes[:2],
            ],
        )
        if layer == layers - 2:
            both, reduced[layer + 1] = lax.optimization_barrier((both, added(pieces)))
        both = swap(both)
        total, both = lax.optimization_barrier((turned_local(agg, upstream), both))
        arriving = share(both[:, :own_slots])
        reduced[layer] = added(both[:, own_slots:])
    own = jnp.concatenate(reduced)
    full = swap(jnp.broadcast_to(own[None], (peers, *own.shape)))
    (feat_grad,) = call(
        last_kernel,
        [far(shape((rows, width), F32))],
        [count, near(send_row), *map(near, arriving), near(total)],
        slot_flops,
        "last",
    )
    full = full.reshape(peers, layers, piece, width).swapaxes(0, 1).reshape(layers, 3, width, hidden_width)
    full = full.swapaxes(0, 1).astype(F32)
    return (final, feat_grad, full[0], full[1], full[2])


def solution(mesh):
    return jax.shard_map(
        local,
        mesh=mesh,
        in_specs=(
            P(("groups", "dom"), None),
            P(("groups", "dom")),
            P(("groups", "dom"), None),
            P(("groups", "dom"), None, None, None),
            P(("groups", "dom"), None, None),
            P(("groups", "dom"), None),
            P(("groups", "dom"), None, None),
            P(None, None, "mp"),
            P(None, None, "mp"),
            P(None, "mp", None),
            P(("groups", "dom"), None),
        ),
        out_specs=(
            P(("groups", "dom"), None),
            P(("groups", "dom"), None),
            P("groups", None, "mp"),
            P("groups", None, "mp"),
            P("groups", "mp", None),
        ),
        check_vma=False,
    )
```

```python
import functools

import jax
import jax.numpy as jnp
from jax import lax
from jax.experimental import pallas as pl
from jax.experimental.pallas import tpu as pltpu
from jax.sharding import PartitionSpec as P

BF16 = jnp.bfloat16
F32 = jnp.float32
LANES = 128
BLOCK = 128
SMEM = pl.BlockSpec(memory_space=pltpu.SMEM)
SUB = 512
SLOTS = 512
GRANT = 48 * 1024 * 1024
TILE_COPIES = 3


def shape(dims, dtype):
    return jax.ShapeDtypeStruct(tuple(dims), dtype)


class Layer:
    def __init__(self, index):
        self.index = index


class Traffic:
    def __init__(self, ins, outs, in_sems, out_sems, late):
        self.ins, self.outs, self.in_sems, self.out_sems = ins, outs, in_sems, out_sems
        self.leaving = []
        for k in sorted(range(len(ins)), key=lambda k: late(k)):
            if self.moves(k):
                self.arriving(k).start()

    def moves(self, k):
        return self.ins[k][2] not in ("near", "later")

    def arriving(self, k):
        far, near, cut = self.ins[k]
        source = far.at[cut.index] if isinstance(cut, Layer) else far
        return pltpu.make_async_copy(source, near, self.in_sems.at[k])

    def need(self, *names):
        for k, (_, near, _) in enumerate(self.ins):
            if self.moves(k) and any(near is name for name in names):
                self.arriving(k).wait()

    def put(self, k):
        near, far, cut = self.outs[k]
        if cut != "near":
            copy = pltpu.make_async_copy(near, far, self.out_sems.at[k])
            copy.start()
            self.leaving.append(copy)

    def finish(self):
        for copy in self.leaving:
            copy.wait()


def call(kernel, outs, ins, flops, name, scratch=()):
    moved = sum(x.size * x.dtype.itemsize for x, _ in (*ins, *outs))
    far_ins = [(x, cut) for x, cut in ins if cut is not None]
    scalars = len(ins) - len(far_ins)
    staged = [k for k, (_, cut) in enumerate(far_ins) if cut not in ("near", "later")]
    staged_outs = [k for k, (_, cut) in enumerate(outs) if cut not in ("near", "later")]

    def body(*refs):
        fixed, refs = refs[:scalars], refs[scalars:]
        far_in, refs = refs[: len(far_ins)], refs[len(far_ins) :]
        far_out, refs = refs[: len(outs)], refs[len(outs) :]
        near_in, near_out = list(far_in), list(far_out)
        for k in staged:
            near_in[k], *refs = refs
        for k in staged_outs:
            near_out[k], *refs = refs
        in_sems, out_sems, *own = refs
        traffic = Traffic(
            [(f, n, cut) for f, n, (_, cut) in zip(far_in, near_in, far_ins)],
            [(n, f, cut) for n, f, (_, cut) in zip(near_out, far_out, outs)],
            in_sems,
            out_sems,
            lambda k: far_ins[k][0].shape[-1] == LANES,
        )
        shown = [near_out[k] for k in range(len(outs)) if outs[k][1] != "later"]
        kernel(traffic, *fixed, *near_in, *shown, *own)
        traffic.finish()

    def held(x, cut):
        if cut == "scalars":
            return pltpu.SMEM(x.shape, x.dtype)
        return pltpu.VMEM(x.shape[1:] if isinstance(cut, Layer) else x.shape, x.dtype)

    def space(cut):
        return pltpu.VMEM if cut == "near" else pltpu.HBM

    return pl.pallas_call(
        body,
        out_shape=[space(cut)(x.shape, x.dtype) for x, cut in outs],
        in_specs=[SMEM] * scalars + [pl.BlockSpec(memory_space=space(cut)) for _, cut in far_ins],
        out_specs=[pl.BlockSpec(memory_space=space(cut)) for _, cut in outs],
        scratch_shapes=[
            *(held(*far_ins[k]) for k in staged),
            *(held(*outs[k]) for k in staged_outs),
            pltpu.SemaphoreType.DMA((len(far_ins),)),
            pltpu.SemaphoreType.DMA((len(outs),)),
            *scratch,
        ],
        cost_estimate=pl.CostEstimate(flops=flops, bytes_accessed=moved, transcendentals=0),
        compiler_params=pltpu.CompilerParams(vmem_limit_bytes=GRANT),
        name=name,
    )(
        *[x for x, _ in ins[:scalars]],
        *[pltpu.with_memory_space_constraint(x, space(cut)) for x, cut in far_ins],
    )


def pieces_of(rows):
    size = SUB if rows % SUB == 0 else BLOCK
    return [slice(first, first + size) for first in range(0, rows, size)]


def mm(a, b):
    return jnp.dot(a, b, preferred_element_type=F32)


def mm_t(a, b):
    return lax.dot_general(a, b, (((1,), (1,)), ((), ())), preferred_element_type=F32)


def mm_rows(a, b):
    return lax.dot_general(a, b, (((0,), (0,)), ((), ())), preferred_element_type=F32)


def live(count_ref, start, rows, width):
    index = lax.broadcasted_iota(jnp.int32, (rows, width), 0) + start
    return index < count_ref[0]


def fill_columns(col_ref, list_ref, used):
    peers, n = list_ref.shape[1:]
    w = col_ref.shape[0] // peers
    down = lax.broadcasted_iota(jnp.int32, (w, n), 0) + lax.axis_index("mp") * w
    across = lax.broadcasted_iota(jnp.int32, (w, n), 1)

    def step(q, carry):
        line = jnp.broadcast_to(list_ref[0, pl.ds(q, 1), :], (w, n))
        kept = (down == across) & used(q, across, line)
        col = jnp.sum(jnp.where(kept, line + 1, 0), axis=1, keepdims=True) - 1
        col_ref[pl.ds(pl.multiple_of(q * w, w), w), :] = jnp.broadcast_to(col, (w, LANES))
        return carry

    lax.fori_loop(0, peers, step, 0, unroll=4)


def fill_row(parts, row_ref, list_ref, used):
    peers, n = list_ref.shape[1:]
    w = n // parts
    across = lax.broadcasted_iota(jnp.int32, (1, n), 1)
    me = lax.axis_index("mp")
    for q in range(peers):
        line = list_ref[0, q : q + 1, :]
        line = jnp.where(used(q, across, line), line, -1)
        for t in range(parts):
            owner = lax.rem(me + t, parts)
            piece = line[:, :w]
            for p in range(1, parts):
                piece = jnp.where(owner == p, line[:, p * w : (p + 1) * w], piece)
            row_ref[0:1, (t * peers + q) * w : (t * peers + q + 1) * w] = piece


def sent(count_ref, used_ref):
    return lambda q, k, row: (k < used_ref[0, q]) & (row < count_ref[0])


def always(q, k, row):
    return row >= 0


def picks(col, rows):
    lanes = lax.broadcasted_iota(jnp.int32, col.shape, 1)
    return jnp.concatenate(
        [jnp.where(col == lanes + lane, 1.0, 0.0).astype(BF16) for lane in range(0, rows, LANES)], axis=1
    )


def gather_rows(col_ref, source_ref, out_ref):
    slots, rows = out_ref.shape[0], source_ref.shape[0]
    size = min(slots, SLOTS)
    for first in range(0, slots, size):
        at = slice(first, first + size)
        out_ref[at, :] = mm(picks(col_ref[at, :], rows), source_ref[...]).astype(BF16)


def scatter_rows(row_ref, start, rows, arriving):
    slots = row_ref.shape[1] // len(arriving)
    index = lax.broadcasted_iota(jnp.int32, (rows, slots), 0) + start
    total = None
    for t, ref in enumerate(arriving):
        pick = jnp.where(row_ref[0:1, t * slots : (t + 1) * slots] == index, 1.0, 0.0).astype(BF16)
        total = mm(pick, ref[...]) if total is None else total + mm(pick, ref[...])
    return total


def send_kernel(traffic, count_ref, used_ref, list_ref, feats_ref, out_ref, col_ref, pick_ref):
    traffic.need(used_ref, list_ref)
    fill_columns(col_ref, list_ref, sent(count_ref, used_ref))
    traffic.put(1)
    pick_ref[...] = picks(col_ref[...], feats_ref.shape[0])
    traffic.need(feats_ref)
    out_ref[...] = mm(pick_ref[...], feats_ref[...]).astype(BF16)
    traffic.put(0)


class Dense:
    def __init__(self, cols_ref, tile_ref, near_ref, dense_ref, sems):
        self.cols_ref, self.near_ref, self.dense_ref = cols_ref, near_ref, dense_ref
        pieces = sems.shape[0]
        self.size = tile_ref.shape[0] // pieces
        self.copies = [
            pltpu.make_async_copy(
                tile_ref.at[pl.ds(p * self.size, self.size)], near_ref.at[pl.ds(p * self.size, self.size)], sems.at[p]
            )
            for p in range(pieces)
        ]
        for copy in self.copies:
            copy.start()

    def zero(self):
        self.dense_ref[...] = jnp.zeros_like(self.dense_ref)

    def fill(self, p):
        self.copies[p].wait()
        for r in range(p * self.size, (p + 1) * self.size):
            for j in range(self.near_ref.shape[1]):
                at = pl.ds(pl.multiple_of(self.cols_ref[r, j] * BLOCK, BLOCK), BLOCK)
                self.dense_ref[r * BLOCK : (r + 1) * BLOCK, at] = self.near_ref[r, j]


def local_sums(traffic, dense, state_ref, sum_ref, out):
    for p in range(len(dense.copies)):
        dense.fill(p)
    sum_ref[...] = mm(dense.dense_ref[...], state_ref[...]).astype(sum_ref.dtype)
    traffic.put(out)


def first_local_kernel(
    parts, traffic, count_ref, used_ref, cols_ref, send_ref, recv_ref, feats_ref, tile_ref,
    sum_ref, send_row_ref, recv_row_ref, recv_col_ref, near_ref, dense_ref, sems, state_ref,
):
    dense = Dense(cols_ref, tile_ref, near_ref, dense_ref, sems)
    rows, width = feats_ref.shape
    traffic.need(send_ref, recv_ref)
    fill_row(parts, send_row_ref, send_ref, sent(count_ref, used_ref))
    fill_row(parts, recv_row_ref, recv_ref, always)
    fill_columns(recv_col_ref, recv_ref, always)
    dense.zero()
    traffic.need(feats_ref)
    state_ref[...] = jnp.where(live(count_ref, 0, rows, width), feats_ref[...], jnp.zeros((), BF16))
    for k in (1, 2, 3):
        traffic.put(k)
    local_sums(traffic, dense, state_ref, sum_ref, 0)


def local_kernel(traffic, cols_ref, state_ref, tile_ref, sum_ref, near_ref, dense_ref, sems):
    dense = Dense(cols_ref, tile_ref, near_ref, dense_ref, sems)
    dense.zero()
    local_sums(traffic, dense, state_ref, sum_ref, 0)


def turned_local_kernel(traffic, count_ref, cols_ref, agg_ref, up_ref, tile_ref, sum_ref, near_ref, dense_ref, sems):
    dense = Dense(cols_ref, tile_ref, near_ref, dense_ref, sems)
    dense.zero()
    for p in range(len(dense.copies)):
        dense.fill(p)
    traffic.need(up_ref)
    upstream = jnp.where(live(count_ref, 0, *sum_ref.shape), up_ref[...].astype(F32), 0.0)
    sum_ref[...] = (mm_rows(dense_ref[...], agg_ref[...]) + upstream).astype(sum_ref.dtype)
    traffic.put(0)


def triples(refs, layer):
    return [(refs[i].at[layer], refs[i + 1].at[layer], refs[i + 2]) for i in range(0, len(refs), 3)]


def gates(acts, weights):
    result = []
    for gate_ref, up_ref, _ in weights:
        gate = mm(acts, gate_ref[...])
        up = mm(acts, up_ref[...])
        sig = 0.5 * jnp.tanh(0.5 * gate) + 0.5
        result.append((gate, up, sig, gate * sig))
    return result


def layer_grads(at, acts, terms, down_in, weights, agg_ref, kept):
    agg = None
    for part, ((gate, up, sig, silu), (gate_ref, up_ref, down_ref)) in enumerate(zip(terms, weights)):
        hidden_grad = mm_t(down_in, down_ref[...])
        slope = sig + silu * (1.0 - sig)
        gate_grad = (hidden_grad * up * slope).astype(BF16)
        up_grad = (hidden_grad * silu).astype(BF16)
        more = mm_t(gate_grad, gate_ref[...]) + mm_t(up_grad, up_ref[...])
        agg = more if agg is None else agg + more
        if part == 0:
            hidden_ref, both_ref, *down = kept
            half = gate_grad.shape[1]
            hidden_ref[at, :] = (silu * up).astype(BF16)
            both_ref[at, :half] = gate_grad
            both_ref[at, half:] = up_grad
            for ref in down:
                ref[at, :] = down_in
    agg_ref[at, :] = agg.astype(BF16)


def weight_grads(acts_ref, kept, dw_ref):
    hidden_ref, both_ref, down_ref = kept
    size = acts_ref.shape[1]
    half = both_ref.shape[1] // 2
    both = mm_rows(acts_ref[...], both_ref[...]).astype(BF16)
    dw_ref[:size, :] = both[:, :half]
    dw_ref[size : 2 * size, :] = both[:, half:]
    dw_ref[2 * size :, :] = mm_rows(hidden_ref[...], down_ref[...]).astype(BF16)


def mix(terms, weights):
    mixed = None
    for (gate, up, sig, silu), (_, _, down_ref) in zip(terms, weights):
        part = mm((silu * up).astype(BF16), down_ref[...])
        mixed = part if mixed is None else mixed + part
    return mixed


def forward_kernel(parts, layer, traffic, count_ref, col_ref, row_ref, *refs):
    arriving, refs = refs[:parts], refs[parts:]
    weights = triples(refs[: 3 * parts], layer)
    sum_ref, state_ref, acts_ref, next_ref, out_ref = refs[3 * parts :]
    width = state_ref.shape[1]
    for at in pieces_of(state_ref.shape[0]):
        size = at.stop - at.start
        acts = (sum_ref[at, :].astype(F32) + scatter_rows(row_ref, at.start, size, arriving)).astype(BF16)
        acts_ref[at, :] = acts
        terms = gates(acts, weights)
        if at.start == 0:
            traffic.need(*(down_ref for _, _, down_ref in weights), state_ref)
        after = state_ref[at, :].astype(F32) + mix(terms, weights)
        next_ref[at, :] = jnp.where(live(count_ref, at.start, size, width), after, 0.0).astype(BF16)
    traffic.put(0)
    traffic.need(col_ref)
    gather_rows(col_ref, next_ref, out_ref)
    traffic.put(2)


def turn_kernel(parts, layer, paired, traffic, count_ref, col_ref, row_ref, *refs):
    arriving, refs = refs[:parts], refs[parts:]
    weights = triples(refs[: 3 * parts], layer)
    sum_ref, state_ref, grad_ref, final_ref, agg_ref, out_ref, *refs = refs[3 * parts :]
    if paired:
        acts_ref, *kept, dw_ref, sems = refs
    else:
        dw_ref, acts_ref, *kept = refs
    width = state_ref.shape[1]
    for at in pieces_of(state_ref.shape[0]):
        size = at.stop - at.start
        acts = (sum_ref[at, :].astype(F32) + scatter_rows(row_ref, at.start, size, arriving)).astype(BF16)
        acts_ref[at, :] = acts
        terms = gates(acts, weights)
        if at.start == 0:
            traffic.need(*(down_ref for _, _, down_ref in weights), state_ref)
        after = state_ref[at, :].astype(F32) + mix(terms, weights)
        alive = live(count_ref, at.start, size, width)
        final_ref[at, :] = jnp.where(alive, after, 0.0).astype(BF16)
        if at.start == 0:
            traffic.need(grad_ref)
        down_in = jnp.where(alive, grad_ref[at, :], jnp.zeros((), BF16))
        layer_grads(at, acts, terms, down_in, weights, agg_ref, kept)
    traffic.put(0)
    traffic.need(col_ref)
    gather_rows(col_ref, agg_ref, out_ref)
    traffic.put(2)
    weight_grads(acts_ref, kept, dw_ref)
    if paired:
        put_halves(traffic, 3, dw_ref, sems)
    else:
        traffic.put(3)


def put_halves(traffic, k, source, sems):
    half = source.shape[0] // 2
    mine = lax.rem(lax.axis_index("dom"), 2)
    for j, which in enumerate((mine, 1 - mine)):
        at = pl.ds(pl.multiple_of(which * half, half), half)
        copy = pltpu.make_async_copy(source.at[at], traffic.outs[k + j][1], sems.at[j])
        copy.start()
        traffic.leaving.append(copy)


def put_pieces(traffic, k, first, source, sems):
    far = traffic.outs[k][1]
    rows = source.shape[0] // far.shape[0]
    for q in range(far.shape[0]):
        copy = pltpu.make_async_copy(source.at[pl.ds(q * rows, rows)], far.at[q, pl.ds(first, rows)], sems.at[q])
        copy.start()
        traffic.leaving.append(copy)
    return first + rows


def backward_kernel(parts, layer, counts, traffic, count_ref, col_ref, row_ref, *refs):
    arriving, refs = refs[:parts], refs[parts:]
    weights = triples(refs[: 3 * parts], layer)
    sum_ref, acts_ref, *refs = refs[3 * parts :]
    earlier, refs = refs[: sum(counts)], refs[sum(counts) :]
    upstream_ref, agg_ref, out_ref, dw_ref, *refs = refs
    if counts:
        added, sems, kept = refs[: len(counts)], refs[len(counts)], refs[len(counts) + 1 :]
    else:
        kept = refs
    rows, width = acts_ref.shape
    for at in pieces_of(rows):
        size = at.stop - at.start
        carried = sum_ref[at, :].astype(F32) + scatter_rows(row_ref, at.start, size, arriving)
        upstream_ref[at, :] = jnp.where(live(count_ref, at.start, size, width), carried, 0.0).astype(BF16)
    traffic.put(0)
    traffic.need(acts_ref, *(down_ref for _, _, down_ref in weights))
    for at in pieces_of(rows):
        acts = acts_ref[at, :]
        layer_grads(at, acts, gates(acts, weights), upstream_ref[at, :], weights, agg_ref, kept)
    traffic.need(col_ref, *earlier)
    gather_rows(col_ref, agg_ref, out_ref)
    if not counts:
        traffic.put(2)
        weight_grads(acts_ref, (*kept, upstream_ref), dw_ref)
        traffic.put(3)
        return
    first = put_pieces(traffic, 2, 0, out_ref, sems.at[0])
    taken = 0
    for k, count in enumerate(counts):
        total = earlier[taken][...].astype(F32)
        for ref in earlier[taken + 1 : taken + count]:
            total = total + ref[...].astype(F32)
        added[k][...] = total.astype(BF16)
        taken += count
        first = put_pieces(traffic, 2, first, added[k], sems.at[1 + k])
    weight_grads(acts_ref, (*kept, upstream_ref), dw_ref)
    put_pieces(traffic, 2, first, dw_ref, sems.at[1 + len(counts)])


def last_kernel(traffic, count_ref, row_ref, *refs):
    *arriving, sum_ref, out_ref = refs
    width = out_ref.shape[1]
    for at in pieces_of(out_ref.shape[0]):
        size = at.stop - at.start
        carried = sum_ref[at, :].astype(F32) + scatter_rows(row_ref, at.start, size, arriving)
        out_ref[at, :] = jnp.where(live(count_ref, at.start, size, width), carried, 0.0)
    traffic.put(0)


def local(
    feats,
    cell_count,
    tile_col,
    tile_val,
    send_list,
    send_count,
    recv_list,
    gate_weight_matrix,
    w_up,
    w_down,
    out_grad,
):
    rows, width = feats.shape
    peers, slot_count = send_list.shape[1:]
    slots = peers * slot_count
    layers = gate_weight_matrix.shape[0]
    hidden_width = gate_weight_matrix.shape[2]
    parts = lax.axis_size("mp")

    turns = [[(d, (d - t) % parts) for d in range(parts)] for t in range(1, parts)]

    def swap(blocks):
        return lax.all_to_all(blocks, "dom", split_axis=0, concat_axis=0, tiled=True)

    def share(rows):
        rows = rows.reshape(slots // parts, width)
        return [rows] + [lax.ppermute(rows, "mp", turn) for turn in turns]

    def exchange(outgoing):
        return swap(outgoing.reshape(peers, slot_count // parts, width))

    def share_after(total, moved):
        total, moved = lax.optimization_barrier((total, moved))
        return total, share(moved)

    def far(x):
        return x, "far"

    def near(x):
        return x, "near"

    state_shape, sum_shape = shape((rows, width), BF16), shape((rows, width), BF16)
    slot_shape = shape((slots // parts, width), BF16)
    dense_scratch = [
        pltpu.VMEM(tile_val.shape, BF16),
        pltpu.VMEM((rows, rows), BF16),
        pltpu.SemaphoreType.DMA((TILE_COPIES,)),
    ]
    tiles, cols = (tile_val, "later"), (tile_col, None)
    row_shape, col_shape = shape((1, slots), jnp.int32), shape((slots // parts, LANES), jnp.int32)
    dw_shape = shape((3 * width, hidden_width), BF16)
    half = pltpu.VMEM((rows, hidden_width), BF16)
    kept_shapes = [half, pltpu.VMEM((rows, 2 * hidden_width), BF16), pltpu.VMEM((rows, width), BF16)]
    local_flops = 2 * rows * rows * width
    slot_flops = 2 * rows * slots * width
    layer_flops = 6 * rows * width * hidden_width * parts
    count = (cell_count, None)

    outgoing, send_col = call(
        send_kernel,
        [far(slot_shape), far(col_shape)],
        [count, (send_count, "scalars"), far(send_list), far(feats)],
        slot_flops,
        "send",
        [pltpu.VMEM((slots // parts, rows), BF16)],
    )
    outgoing, mine = lax.optimization_barrier((outgoing, (gate_weight_matrix, w_up, w_down)))
    arriving = exchange(outgoing)
    held = [mine] + [tuple(lax.ppermute(w, "mp", turn) for w in mine) for turn in turns]

    def weights(layer):
        return [spec for gate, up, down in held for spec in (near(gate), near(up), (down, Layer(layer)))]

    total, send_row, recv_row, recv_col = call(
        functools.partial(first_local_kernel, parts),
        [
            near(sum_shape),
            near(row_shape),
            near(row_shape),
            far(col_shape),
        ],
        [
            count,
            (send_count, None),
            cols,
            far(send_list),
            far(recv_list),
            far(feats),
            tiles,
        ],
        local_flops,
        "first_local",
        [*dense_scratch, pltpu.VMEM((rows, width), BF16)],
    )
    total, arriving = share_after(total, arriving)
    state = far(feats)
    kept = []
    for layer in range(layers - 1):
        acts, after, outgoing = call(
            functools.partial(forward_kernel, parts, layer),
            [far(state_shape), near(state_shape), far(slot_shape)],
            [count, far(send_col), near(recv_row), *map(near, arriving), *weights(layer), near(total), state],
            layer_flops + 2 * slot_flops,
            "forward",
        )
        kept.append(acts)
        state = near(after)
        arriving = exchange(outgoing)
        (total,) = call(
            local_kernel, [near(sum_shape)], [cols, state, tiles], local_flops, "local", dense_scratch
        )
        total, arriving = share_after(total, arriving)
    half_dw = shape((dw_shape.shape[0] // 2, width), BF16)
    paired = peers % 2 == 0 and layers > 1 and half_dw.shape[0] % (16 * peers) == 0
    dw_scratch = pltpu.VMEM(dw_shape.shape, BF16)
    final, agg, outgoing, *dw = call(
        functools.partial(turn_kernel, parts, layers - 1, paired),
        [
            far(state_shape), near(state_shape), far(slot_shape),
            *([(half_dw, "later")] * 2 if paired else [far(dw_shape)]),
        ],
        [
            count, far(recv_col), near(recv_row), *map(near, arriving), *weights(layers - 1), near(total),
            state, far(out_grad),
        ],
        3 * layer_flops + 2 * slot_flops,
        "turn",
        [
            pltpu.VMEM((rows, width), BF16),
            *kept_shapes,
            *([dw_scratch, pltpu.SemaphoreType.DMA((2,))] if paired else []),
        ],
    )
    piece = dw_shape.shape[0] // peers
    own_slots = slot_count // parts

    def turned_local(agg, upstream):
        return call(
            turned_local_kernel,
            [near(sum_shape)],
            [count, cols, near(agg), far(upstream), tiles],
            local_flops,
            "turned_local",
            dense_scratch,
        )[0]

    upstream = out_grad
    earlier = []
    for layer in reversed(range(layers - 1)):
        moved = exchange(outgoing)
        if len(dw) == 2:
            dw = [dw[0], lax.ppermute(dw[1], "dom", [(d, d ^ 1) for d in range(peers)])]
        total, arriving = share_after(turned_local(agg, upstream), moved)
        earlier.append(dw)
        bottom = layer == 0
        counts = [len(addends) for addends in earlier] if bottom else []
        lengths = [addends[0].shape[0] for addends in earlier]
        wide = shape((peers, own_slots + sum(lengths) // peers + piece, width), BF16)
        upstream, agg, outgoing, *dw = call(
            functools.partial(backward_kernel, parts, layer, counts),
            [far(sum_shape), near(state_shape), *([(wide, "later")] if bottom else [far(slot_shape), far(dw_shape)])],
            [
                count, far(recv_col), near(send_row), *map(near, arriving), *weights(layer), near(total),
                far(kept[layer]), *(far(x) for addends in earlier for x in addends if bottom),
            ],
            3 * layer_flops + 2 * slot_flops,
            "backward",
            [
                *([pltpu.VMEM(slot_shape.shape, BF16), dw_scratch] if bottom else []),
                *(pltpu.VMEM((n, width), BF16) for n in lengths if bottom),
                *([pltpu.SemaphoreType.DMA((2 + len(counts), peers))] if bottom else []),
                *kept_shapes[:2],
            ],
        )
    total, pieces = lax.optimization_barrier((turned_local(agg, upstream), swap(outgoing)))
    arriving = share(pieces[:, :own_slots])
    sizes = [n // peers for n in lengths] + [piece]
    cuts = [own_slots + sum(sizes[:k]) for k in range(len(sizes))]
    owned = []
    for first, size in zip(cuts, sizes):
        groups = piece // size
        part = pieces[:, first : first + size].astype(F32).reshape(peers // groups, groups * size, width)
        owned.append(jnp.sum(part, axis=0).astype(BF16))
    own = jnp.concatenate(owned)
    full = swap(jnp.broadcast_to(own[None], (peers, *own.shape)))
    (feat_grad,) = call(
        last_kernel,
        [far(shape((rows, width), F32))],
        [count, near(send_row), *map(near, arriving), near(total)],
        slot_flops,
        "last",
    )
    by_layer = []
    for k, size in enumerate(sizes):
        groups = piece // size
        rows_of_layer = full[:, k * piece : (k + 1) * piece].reshape(peers, groups, size, width).swapaxes(0, 1)
        by_layer.append(rows_of_layer.reshape(3, width, hidden_width))
    full = jnp.stack(by_layer[::-1], axis=1).astype(F32)
    return (final, feat_grad, full[0], full[1], full[2])


def solution(mesh):
    return jax.shard_map(
        local,
        mesh=mesh,
        in_specs=(
            P(("groups", "dom"), None),
            P(("groups", "dom")),
            P(("groups", "dom"), None),
            P(("groups", "dom"), None, None, None),
            P(("groups", "dom"), None, None),
            P(("groups", "dom"), None),
            P(("groups", "dom"), None, None),
            P(None, None, "mp"),
            P(None, None, "mp"),
            P(None, "mp", None),
            P(("groups", "dom"), None),
        ),
        out_specs=(
            P(("groups", "dom"), None),
            P(("groups", "dom"), None),
            P("groups", None, "mp"),
            P("groups", None, "mp"),
            P("groups", "mp", None),
        ),
        check_vma=False,
    )
```

```python
import functools

import jax
import jax.numpy as jnp
from jax import lax
from jax.experimental import pallas as pl
from jax.experimental.pallas import tpu as pltpu
from jax.sharding import PartitionSpec as P

BF16 = jnp.bfloat16
F32 = jnp.float32
LANES = 128
BLOCK = 128
SMEM = pl.BlockSpec(memory_space=pltpu.SMEM)
SUB = 512
SLOTS = 512
GRANT = 48 * 1024 * 1024
TILE_COPIES = 2


def shape(dims, dtype):
    return jax.ShapeDtypeStruct(tuple(dims), dtype)


class Layer:
    def __init__(self, index):
        self.index = index


class Traffic:
    def __init__(self, ins, outs, in_sems, out_sems, late):
        self.ins, self.outs, self.in_sems, self.out_sems = ins, outs, in_sems, out_sems
        self.leaving = []
        for k in sorted(range(len(ins)), key=lambda k: late(k)):
            if self.moves(k):
                self.arriving(k).start()

    def moves(self, k):
        return self.ins[k][2] not in ("near", "later")

    def arriving(self, k):
        far, near, cut = self.ins[k]
        source = far.at[cut.index] if isinstance(cut, Layer) else far
        return pltpu.make_async_copy(source, near, self.in_sems.at[k])

    def need(self, *names):
        for k, (_, near, _) in enumerate(self.ins):
            if self.moves(k) and any(near is name for name in names):
                self.arriving(k).wait()

    def put(self, k):
        near, far, cut = self.outs[k]
        if cut != "near":
            copy = pltpu.make_async_copy(near, far, self.out_sems.at[k])
            copy.start()
            self.leaving.append(copy)

    def finish(self):
        for copy in self.leaving:
            copy.wait()


def call(kernel, outs, ins, flops, name, scratch=()):
    moved = sum(x.size * x.dtype.itemsize for x, _ in (*ins, *outs))
    far_ins = [(x, cut) for x, cut in ins if cut is not None]
    scalars = len(ins) - len(far_ins)
    staged = [k for k, (_, cut) in enumerate(far_ins) if cut not in ("near", "later")]
    staged_outs = [k for k, (_, cut) in enumerate(outs) if cut not in ("near", "later")]

    def body(*refs):
        fixed, refs = refs[:scalars], refs[scalars:]
        far_in, refs = refs[: len(far_ins)], refs[len(far_ins) :]
        far_out, refs = refs[: len(outs)], refs[len(outs) :]
        near_in, near_out = list(far_in), list(far_out)
        for k in staged:
            near_in[k], *refs = refs
        for k in staged_outs:
            near_out[k], *refs = refs
        in_sems, out_sems, *own = refs
        traffic = Traffic(
            [(f, n, cut) for f, n, (_, cut) in zip(far_in, near_in, far_ins)],
            [(n, f, cut) for n, f, (_, cut) in zip(near_out, far_out, outs)],
            in_sems,
            out_sems,
            lambda k: far_ins[k][0].shape[-1] == LANES,
        )
        shown = [near_out[k] for k in range(len(outs)) if outs[k][1] != "later"]
        kernel(traffic, *fixed, *near_in, *shown, *own)
        traffic.finish()

    def held(x, cut):
        if cut == "scalars":
            return pltpu.SMEM(x.shape, x.dtype)
        return pltpu.VMEM(x.shape[1:] if isinstance(cut, Layer) else x.shape, x.dtype)

    def space(cut):
        return pltpu.VMEM if cut == "near" else pltpu.HBM

    return pl.pallas_call(
        body,
        out_shape=[space(cut)(x.shape, x.dtype) for x, cut in outs],
        in_specs=[SMEM] * scalars + [pl.BlockSpec(memory_space=space(cut)) for _, cut in far_ins],
        out_specs=[pl.BlockSpec(memory_space=space(cut)) for _, cut in outs],
        scratch_shapes=[
            *(held(*far_ins[k]) for k in staged),
            *(held(*outs[k]) for k in staged_outs),
            pltpu.SemaphoreType.DMA((len(far_ins),)),
            pltpu.SemaphoreType.DMA((len(outs),)),
            *scratch,
        ],
        cost_estimate=pl.CostEstimate(flops=flops, bytes_accessed=moved, transcendentals=0),
        compiler_params=pltpu.CompilerParams(vmem_limit_bytes=GRANT),
        name=name,
    )(
        *[x for x, _ in ins[:scalars]],
        *[pltpu.with_memory_space_constraint(x, space(cut)) for x, cut in far_ins],
    )


def pieces_of(rows):
    size = SUB if rows % SUB == 0 else BLOCK
    return [slice(first, first + size) for first in range(0, rows, size)]


def mm(a, b):
    return jnp.dot(a, b, preferred_element_type=F32)


def mm_t(a, b):
    return lax.dot_general(a, b, (((1,), (1,)), ((), ())), preferred_element_type=F32)


def mm_rows(a, b):
    return lax.dot_general(a, b, (((0,), (0,)), ((), ())), preferred_element_type=F32)


def live(count_ref, start, rows, width):
    index = lax.broadcasted_iota(jnp.int32, (rows, width), 0) + start
    return index < count_ref[0]


def fill_columns(col_ref, list_ref, used):
    peers, n = list_ref.shape[1:]
    w = col_ref.shape[0] // peers
    down = lax.broadcasted_iota(jnp.int32, (w, n), 0) + lax.axis_index("mp") * w
    across = lax.broadcasted_iota(jnp.int32, (w, n), 1)

    def step(q, carry):
        line = jnp.broadcast_to(list_ref[0, pl.ds(q, 1), :], (w, n))
        kept = (down == across) & used(q, across, line)
        col = jnp.sum(jnp.where(kept, line + 1, 0), axis=1, keepdims=True) - 1
        col_ref[pl.ds(pl.multiple_of(q * w, w), w), :] = jnp.broadcast_to(col, (w, LANES))
        return carry

    lax.fori_loop(0, peers, step, 0, unroll=4)


def fill_row(parts, row_ref, list_ref, used):
    peers, n = list_ref.shape[1:]
    w = n // parts
    across = lax.broadcasted_iota(jnp.int32, (1, n), 1)
    me = lax.axis_index("mp")
    for q in range(peers):
        line = list_ref[0, q : q + 1, :]
        line = jnp.where(used(q, across, line), line, -1)
        for t in range(parts):
            owner = lax.rem(me + t, parts)
            piece = line[:, :w]
            for p in range(1, parts):
                piece = jnp.where(owner == p, line[:, p * w : (p + 1) * w], piece)
            row_ref[0:1, (t * peers + q) * w : (t * peers + q + 1) * w] = piece


def sent(count_ref, used_ref):
    return lambda q, k, row: (k < used_ref[0, q]) & (row < count_ref[0])


def always(q, k, row):
    return row >= 0


def picks(col, rows):
    lanes = lax.broadcasted_iota(jnp.int32, col.shape, 1)
    return jnp.concatenate(
        [jnp.where(col == lanes + lane, 1.0, 0.0).astype(BF16) for lane in range(0, rows, LANES)], axis=1
    )


def gather_rows(col_ref, source_ref, out_ref):
    slots, rows = out_ref.shape[0], source_ref.shape[0]
    size = min(slots, SLOTS)
    for first in range(0, slots, size):
        at = slice(first, first + size)
        out_ref[at, :] = mm(picks(col_ref[at, :], rows), source_ref[...]).astype(BF16)


def scatter_rows(row_ref, start, rows, arriving):
    slots = row_ref.shape[1] // len(arriving)
    index = lax.broadcasted_iota(jnp.int32, (rows, slots), 0) + start
    total = None
    for t, ref in enumerate(arriving):
        pick = jnp.where(row_ref[0:1, t * slots : (t + 1) * slots] == index, 1.0, 0.0).astype(BF16)
        total = mm(pick, ref[...]) if total is None else total + mm(pick, ref[...])
    return total


def send_kernel(
    traffic, count_ref, used_ref, list_ref, recv_ref, feats_ref, out_ref, col_ref, recv_col_ref, pick_ref
):
    traffic.need(used_ref, list_ref, recv_ref)
    fill_columns(col_ref, list_ref, sent(count_ref, used_ref))
    traffic.put(1)
    pick_ref[...] = picks(col_ref[...], feats_ref.shape[0])
    fill_columns(recv_col_ref, recv_ref, always)
    traffic.put(2)
    traffic.need(feats_ref)
    out_ref[...] = mm(pick_ref[...], feats_ref[...]).astype(BF16)
    traffic.put(0)


class Dense:
    def __init__(self, cols_ref, tile_ref, near_ref, dense_ref, sems):
        self.cols_ref, self.near_ref, self.dense_ref = cols_ref, near_ref, dense_ref
        pieces = sems.shape[0]
        self.size = tile_ref.shape[0] // pieces
        self.copies = [
            pltpu.make_async_copy(
                tile_ref.at[pl.ds(p * self.size, self.size)], near_ref.at[pl.ds(p * self.size, self.size)], sems.at[p]
            )
            for p in range(pieces)
        ]
        for copy in self.copies:
            copy.start()

    def zero(self):
        self.dense_ref[...] = jnp.zeros_like(self.dense_ref)

    def fill(self, p):
        self.copies[p].wait()
        for r in range(p * self.size, (p + 1) * self.size):
            for j in range(self.near_ref.shape[1]):
                at = pl.ds(pl.multiple_of(self.cols_ref[r, j] * BLOCK, BLOCK), BLOCK)
                self.dense_ref[r * BLOCK : (r + 1) * BLOCK, at] = self.near_ref[r, j]


def local_sums(traffic, dense, state_ref, sum_ref, out):
    for p in range(len(dense.copies)):
        dense.fill(p)
    sum_ref[...] = mm(dense.dense_ref[...], state_ref[...]).astype(sum_ref.dtype)
    traffic.put(out)


def first_local_kernel(
    parts, traffic, count_ref, used_ref, cols_ref, send_ref, recv_ref, feats_ref, tile_ref,
    sum_ref, send_row_ref, recv_row_ref, near_ref, dense_ref, sems, state_ref,
):
    dense = Dense(cols_ref, tile_ref, near_ref, dense_ref, sems)
    rows, width = feats_ref.shape
    traffic.need(send_ref, recv_ref)
    fill_row(parts, send_row_ref, send_ref, sent(count_ref, used_ref))
    fill_row(parts, recv_row_ref, recv_ref, always)
    dense.zero()
    traffic.need(feats_ref)
    state_ref[...] = jnp.where(live(count_ref, 0, rows, width), feats_ref[...], jnp.zeros((), BF16))
    local_sums(traffic, dense, state_ref, sum_ref, 0)


def local_kernel(traffic, cols_ref, state_ref, tile_ref, sum_ref, near_ref, dense_ref, sems):
    dense = Dense(cols_ref, tile_ref, near_ref, dense_ref, sems)
    dense.zero()
    local_sums(traffic, dense, state_ref, sum_ref, 0)


def turned_local_kernel(traffic, count_ref, cols_ref, agg_ref, up_ref, tile_ref, sum_ref, near_ref, dense_ref, sems):
    dense = Dense(cols_ref, tile_ref, near_ref, dense_ref, sems)
    dense.zero()
    for p in range(len(dense.copies)):
        dense.fill(p)
    traffic.need(up_ref)
    upstream = jnp.where(live(count_ref, 0, *sum_ref.shape), up_ref[...].astype(F32), 0.0)
    sum_ref[...] = (mm_rows(dense_ref[...], agg_ref[...]) + upstream).astype(sum_ref.dtype)
    traffic.put(0)


def triples(refs, layer):
    return [(refs[i].at[layer], refs[i + 1].at[layer], refs[i + 2]) for i in range(0, len(refs), 3)]


def gates(acts, weights):
    result = []
    for gate_ref, up_ref, _ in weights:
        gate = mm(acts, gate_ref[...])
        up = mm(acts, up_ref[...])
        sig = 0.5 * jnp.tanh(0.5 * gate) + 0.5
        result.append((gate, up, sig, gate * sig))
    return result


def layer_grads(at, acts, terms, down_in, weights, agg_ref, kept):
    agg = None
    for part, ((gate, up, sig, silu), (gate_ref, up_ref, down_ref)) in enumerate(zip(terms, weights)):
        hidden_grad = mm_t(down_in, down_ref[...])
        slope = sig + silu * (1.0 - sig)
        gate_grad = (hidden_grad * up * slope).astype(BF16)
        up_grad = (hidden_grad * silu).astype(BF16)
        more = mm_t(gate_grad, gate_ref[...]) + mm_t(up_grad, up_ref[...])
        agg = more if agg is None else agg + more
        if part == 0:
            hidden_ref, both_ref, *down = kept
            half = gate_grad.shape[1]
            hidden_ref[at, :] = (silu * up).astype(BF16)
            both_ref[at, :half] = gate_grad
            both_ref[at, half:] = up_grad
            for ref in down:
                ref[at, :] = down_in
    agg_ref[at, :] = agg.astype(BF16)


def weight_grads(acts_ref, kept, dw_ref):
    hidden_ref, both_ref, down_ref = kept
    size = acts_ref.shape[1]
    half = both_ref.shape[1] // 2
    both = mm_rows(acts_ref[...], both_ref[...]).astype(BF16)
    dw_ref[:size, :] = both[:, :half]
    dw_ref[size : 2 * size, :] = both[:, half:]
    dw_ref[2 * size :, :] = mm_rows(hidden_ref[...], down_ref[...]).astype(BF16)


def mix(terms, weights):
    mixed = None
    for (gate, up, sig, silu), (_, _, down_ref) in zip(terms, weights):
        part = mm((silu * up).astype(BF16), down_ref[...])
        mixed = part if mixed is None else mixed + part
    return mixed


def forward_kernel(parts, layer, traffic, count_ref, col_ref, row_ref, *refs):
    arriving, refs = refs[:parts], refs[parts:]
    weights = triples(refs[: 3 * parts], layer)
    sum_ref, state_ref, acts_ref, next_ref, out_ref = refs[3 * parts :]
    width = state_ref.shape[1]
    for at in pieces_of(state_ref.shape[0]):
        size = at.stop - at.start
        acts = (sum_ref[at, :].astype(F32) + scatter_rows(row_ref, at.start, size, arriving)).astype(BF16)
        acts_ref[at, :] = acts
        terms = gates(acts, weights)
        if at.start == 0:
            traffic.need(*(down_ref for _, _, down_ref in weights), state_ref)
        after = state_ref[at, :].astype(F32) + mix(terms, weights)
        next_ref[at, :] = jnp.where(live(count_ref, at.start, size, width), after, 0.0).astype(BF16)
    traffic.put(0)
    traffic.need(col_ref)
    gather_rows(col_ref, next_ref, out_ref)
    traffic.put(2)


def turn_kernel(parts, layer, paired, traffic, count_ref, col_ref, row_ref, *refs):
    arriving, refs = refs[:parts], refs[parts:]
    weights = triples(refs[: 3 * parts], layer)
    sum_ref, state_ref, grad_ref, final_ref, agg_ref, out_ref, *refs = refs[3 * parts :]
    if paired:
        acts_ref, *kept, dw_ref, sems = refs
    else:
        dw_ref, acts_ref, *kept = refs
    width = state_ref.shape[1]
    for at in pieces_of(state_ref.shape[0]):
        size = at.stop - at.start
        acts = (sum_ref[at, :].astype(F32) + scatter_rows(row_ref, at.start, size, arriving)).astype(BF16)
        acts_ref[at, :] = acts
        terms = gates(acts, weights)
        if at.start == 0:
            traffic.need(*(down_ref for _, _, down_ref in weights), state_ref)
        after = state_ref[at, :].astype(F32) + mix(terms, weights)
        alive = live(count_ref, at.start, size, width)
        final_ref[at, :] = jnp.where(alive, after, 0.0).astype(BF16)
        if at.start == 0:
            traffic.need(grad_ref)
        down_in = jnp.where(alive, grad_ref[at, :], jnp.zeros((), BF16))
        layer_grads(at, acts, terms, down_in, weights, agg_ref, kept)
    traffic.put(0)
    traffic.need(col_ref)
    gather_rows(col_ref, agg_ref, out_ref)
    traffic.put(2)
    weight_grads(acts_ref, kept, dw_ref)
    if paired:
        put_halves(traffic, 3, dw_ref, sems)
    else:
        traffic.put(3)


def put_halves(traffic, k, source, sems):
    half = source.shape[0] // 2
    mine = lax.rem(lax.axis_index("dom"), 2)
    for j, which in enumerate((mine, 1 - mine)):
        at = pl.ds(pl.multiple_of(which * half, half), half)
        copy = pltpu.make_async_copy(source.at[at], traffic.outs[k + j][1], sems.at[j])
        copy.start()
        traffic.leaving.append(copy)


def put_pieces(traffic, k, first, source, sems):
    far = traffic.outs[k][1]
    rows = source.shape[0] // far.shape[0]
    for q in range(far.shape[0]):
        copy = pltpu.make_async_copy(source.at[pl.ds(q * rows, rows)], far.at[q, pl.ds(first, rows)], sems.at[q])
        copy.start()
        traffic.leaving.append(copy)
    return first + rows


def backward_kernel(parts, layer, counts, traffic, count_ref, col_ref, row_ref, *refs):
    arriving, refs = refs[:parts], refs[parts:]
    weights = triples(refs[: 3 * parts], layer)
    sum_ref, acts_ref, *refs = refs[3 * parts :]
    earlier, refs = refs[: sum(counts)], refs[sum(counts) :]
    upstream_ref, agg_ref, out_ref, dw_ref, *refs = refs
    if counts:
        added, sems, kept = refs[: len(counts)], refs[len(counts)], refs[len(counts) + 1 :]
    else:
        kept = refs
    rows, width = acts_ref.shape
    for at in pieces_of(rows):
        size = at.stop - at.start
        carried = sum_ref[at, :].astype(F32) + scatter_rows(row_ref, at.start, size, arriving)
        upstream_ref[at, :] = jnp.where(live(count_ref, at.start, size, width), carried, 0.0).astype(BF16)
    traffic.put(0)
    traffic.need(acts_ref, *(down_ref for _, _, down_ref in weights))
    for at in pieces_of(rows):
        acts = acts_ref[at, :]
        layer_grads(at, acts, gates(acts, weights), upstream_ref[at, :], weights, agg_ref, kept)
    traffic.need(col_ref, *earlier)
    gather_rows(col_ref, agg_ref, out_ref)
    if not counts:
        traffic.put(2)
        weight_grads(acts_ref, (*kept, upstream_ref), dw_ref)
        traffic.put(3)
        return
    first = put_pieces(traffic, 2, 0, out_ref, sems.at[0])
    taken = 0
    for k, count in enumerate(counts):
        total = earlier[taken][...].astype(F32)
        for ref in earlier[taken + 1 : taken + count]:
            total = total + ref[...].astype(F32)
        added[k][...] = total.astype(BF16)
        taken += count
        first = put_pieces(traffic, 2, first, added[k], sems.at[1 + k])
    weight_grads(acts_ref, (*kept, upstream_ref), dw_ref)
    put_pieces(traffic, 2, first, dw_ref, sems.at[1 + len(counts)])


def last_kernel(traffic, count_ref, row_ref, *refs):
    *arriving, sum_ref, out_ref = refs
    width = out_ref.shape[1]
    for at in pieces_of(out_ref.shape[0]):
        size = at.stop - at.start
        carried = sum_ref[at, :].astype(F32) + scatter_rows(row_ref, at.start, size, arriving)
        out_ref[at, :] = jnp.where(live(count_ref, at.start, size, width), carried, 0.0)
    traffic.put(0)


def local(
    feats,
    cell_count,
    tile_col,
    tile_val,
    send_list,
    send_count,
    recv_list,
    gate_weight_matrix,
    w_up,
    w_down,
    out_grad,
):
    rows, width = feats.shape
    peers, slot_count = send_list.shape[1:]
    slots = peers * slot_count
    layers = gate_weight_matrix.shape[0]
    hidden_width = gate_weight_matrix.shape[2]
    parts = lax.axis_size("mp")

    turns = [[(d, (d - t) % parts) for d in range(parts)] for t in range(1, parts)]

    def swap(blocks):
        return lax.all_to_all(blocks, "dom", split_axis=0, concat_axis=0, tiled=True)

    def share(rows):
        rows = rows.reshape(slots // parts, width)
        return [rows] + [lax.ppermute(rows, "mp", turn) for turn in turns]

    def exchange(outgoing):
        return swap(outgoing.reshape(peers, slot_count // parts, width))

    def share_after(total, moved):
        total, moved = lax.optimization_barrier((total, moved))
        return total, share(moved)

    def far(x):
        return x, "far"

    def near(x):
        return x, "near"

    state_shape, sum_shape = shape((rows, width), BF16), shape((rows, width), BF16)
    slot_shape = shape((slots // parts, width), BF16)
    dense_scratch = [
        pltpu.VMEM(tile_val.shape, BF16),
        pltpu.VMEM((rows, rows), BF16),
        pltpu.SemaphoreType.DMA((TILE_COPIES,)),
    ]
    tiles, cols = (tile_val, "later"), (tile_col, None)
    row_shape, col_shape = shape((1, slots), jnp.int32), shape((slots // parts, LANES), jnp.int32)
    dw_shape = shape((3 * width, hidden_width), BF16)
    half = pltpu.VMEM((rows, hidden_width), BF16)
    kept_shapes = [half, pltpu.VMEM((rows, 2 * hidden_width), BF16), pltpu.VMEM((rows, width), BF16)]
    local_flops = 2 * rows * rows * width
    slot_flops = 2 * rows * slots * width
    layer_flops = 6 * rows * width * hidden_width * parts
    count = (cell_count, None)

    outgoing, send_col, recv_col = call(
        send_kernel,
        [far(slot_shape), far(col_shape), far(col_shape)],
        [count, (send_count, "scalars"), far(send_list), far(recv_list), far(feats)],
        slot_flops,
        "send",
        [pltpu.VMEM((slots // parts, rows), BF16)],
    )
    outgoing, mine = lax.optimization_barrier((outgoing, (gate_weight_matrix, w_up, w_down)))
    arriving = exchange(outgoing)
    held = [mine] + [tuple(lax.ppermute(w, "mp", turn) for w in mine) for turn in turns]

    def weights(layer):
        return [spec for gate, up, down in held for spec in (near(gate), near(up), (down, Layer(layer)))]

    total, send_row, recv_row = call(
        functools.partial(first_local_kernel, parts),
        [
            near(sum_shape),
            near(row_shape),
            near(row_shape),
        ],
        [
            count,
            (send_count, None),
            cols,
            far(send_list),
            far(recv_list),
            far(feats),
            tiles,
        ],
        local_flops,
        "first_local",
        [*dense_scratch, pltpu.VMEM((rows, width), BF16)],
    )
    total, arriving = share_after(total, arriving)
    state = far(feats)
    kept = []
    for layer in range(layers - 1):
        acts, after, outgoing = call(
            functools.partial(forward_kernel, parts, layer),
            [far(state_shape), near(state_shape), far(slot_shape)],
            [count, far(send_col), near(recv_row), *map(near, arriving), *weights(layer), near(total), state],
            layer_flops + 2 * slot_flops,
            "forward",
        )
        kept.append(acts)
        state = near(after)
        arriving = exchange(outgoing)
        (total,) = call(
            local_kernel, [near(sum_shape)], [cols, state, tiles], local_flops, "local", dense_scratch
        )
        total, arriving = share_after(total, arriving)
    half_dw = shape((dw_shape.shape[0] // 2, width), BF16)
    paired = peers % 2 == 0 and layers > 1 and half_dw.shape[0] % (16 * peers) == 0
    dw_scratch = pltpu.VMEM(dw_shape.shape, BF16)
    final, agg, outgoing, *dw = call(
        functools.partial(turn_kernel, parts, layers - 1, paired),
        [
            far(state_shape), near(state_shape), far(slot_shape),
            *([(half_dw, "later")] * 2 if paired else [far(dw_shape)]),
        ],
        [
            count, far(recv_col), near(recv_row), *map(near, arriving), *weights(layers - 1), near(total),
            state, far(out_grad),
        ],
        3 * layer_flops + 2 * slot_flops,
        "turn",
        [
            pltpu.VMEM((rows, width), BF16),
            *kept_shapes,
            *([dw_scratch, pltpu.SemaphoreType.DMA((2,))] if paired else []),
        ],
    )
    piece = dw_shape.shape[0] // peers
    own_slots = slot_count // parts

    def turned_local(agg, upstream):
        return call(
            turned_local_kernel,
            [near(sum_shape)],
            [count, cols, near(agg), far(upstream), tiles],
            local_flops,
            "turned_local",
            dense_scratch,
        )[0]

    upstream = out_grad
    earlier = []
    for layer in reversed(range(layers - 1)):
        moved = exchange(outgoing)
        if len(dw) == 2:
            dw = [dw[0], lax.ppermute(dw[1], "dom", [(d, d ^ 1) for d in range(peers)])]
        total, arriving = share_after(turned_local(agg, upstream), moved)
        earlier.append(dw)
        bottom = layer == 0
        counts = [len(addends) for addends in earlier] if bottom else []
        lengths = [addends[0].shape[0] for addends in earlier]
        wide = shape((peers, own_slots + sum(lengths) // peers + piece, width), BF16)
        upstream, agg, outgoing, *dw = call(
            functools.partial(backward_kernel, parts, layer, counts),
            [far(sum_shape), near(state_shape), *([(wide, "later")] if bottom else [far(slot_shape), far(dw_shape)])],
            [
                count, far(recv_col), near(send_row), *map(near, arriving), *weights(layer), near(total),
                far(kept[layer]), *(far(x) for addends in earlier for x in addends if bottom),
            ],
            3 * layer_flops + 2 * slot_flops,
            "backward",
            [
                *([pltpu.VMEM(slot_shape.shape, BF16), dw_scratch] if bottom else []),
                *(pltpu.VMEM((n, width), BF16) for n in lengths if bottom),
                *([pltpu.SemaphoreType.DMA((2 + len(counts), peers))] if bottom else []),
                *kept_shapes[:2],
            ],
        )
    total, pieces = lax.optimization_barrier((turned_local(agg, upstream), swap(outgoing)))
    arriving = share(pieces[:, :own_slots])
    sizes = [n // peers for n in lengths] + [piece]
    cuts = [own_slots + sum(sizes[:k]) for k in range(len(sizes))]
    owned = []
    for first, size in zip(cuts, sizes):
        groups = piece // size
        part = pieces[:, first : first + size].astype(F32).reshape(peers // groups, groups * size, width)
        owned.append(jnp.sum(part, axis=0).astype(BF16))
    own = jnp.concatenate(owned)
    full = swap(jnp.broadcast_to(own[None], (peers, *own.shape)))
    (feat_grad,) = call(
        last_kernel,
        [far(shape((rows, width), F32))],
        [count, near(send_row), *map(near, arriving), near(total)],
        slot_flops,
        "last",
    )
    by_layer = []
    for k, size in enumerate(sizes):
        groups = piece // size
        rows_of_layer = full[:, k * piece : (k + 1) * piece].reshape(peers, groups, size, width).swapaxes(0, 1)
        by_layer.append(rows_of_layer.reshape(3, width, hidden_width))
    full = jnp.stack(by_layer[::-1], axis=1).astype(F32)
    return (final, feat_grad, full[0], full[1], full[2])


def solution(mesh):
    return jax.shard_map(
        local,
        mesh=mesh,
        in_specs=(
            P(("groups", "dom"), None),
            P(("groups", "dom")),
            P(("groups", "dom"), None),
            P(("groups", "dom"), None, None, None),
            P(("groups", "dom"), None, None),
            P(("groups", "dom"), None),
            P(("groups", "dom"), None, None),
            P(None, None, "mp"),
            P(None, None, "mp"),
            P(None, "mp", None),
            P(("groups", "dom"), None),
        ),
        out_specs=(
            P(("groups", "dom"), None),
            P(("groups", "dom"), None),
            P("groups", None, "mp"),
            P("groups", None, "mp"),
            P("groups", "mp", None),
        ),
        check_vma=False,
    )
```
